32 devices in a mesh: elem: 2 (over core), band: 16 (over z, y, x).
Axes of the slice: x: 2, y: 2, z: 4, core: 2. Of those that a mesh axis runs over, the one named last changes fastest.
Arguments:
- coefficients: bfloat16 [8, 128, 8192], P('elem', None, 'band'), may hold values from -6 to 6
- hamiltonian: bfloat16 [8, 27, 128, 128], P('elem'), may hold values from -0.0546875 to 0.0546875
- neighbours: int32 [8, 27], P('elem'), may hold values from 0 to 7, as said below
- basis_values: bfloat16 [8, 4096, 128], P('elem'), may hold values from -0.5 to 0.5
Outputs:
- filtered: bfloat16 [8, 128, 8192], P('elem', None, 'band')
- density: float32 [8, 4096], P('elem', 'band')
The draws below stay inside these ranges and needn't reach their ends.
Inputs may be any that keep to these rules, and one draw needn't show every extreme that they name: `neighbours`: elements sit on a periodic grid of 2 x 2 x 2 cells in an order drawn from the seed; row e lists the elements at offsets (dx, dy, dz) in -1..1, with k = 9 (dx + 1) + 3 (dy + 1) + dz + 1.
All inputs are finite; a program needn't handle non-finite values.
Results may differ from the reference program's by a relative error of at most 0.0065.
Values may be sent and summed in bfloat16 or wider, within the bound.
A program may use at most 64 MiB of HBM per device.

```python
import jax
import jax.numpy as jnp
from jax import lax

NB = 128
BANDS = 8192
POINTS = 4096
CHEB = 6
ELEMS = 8


def draw_neighbours(key, part):
    mixed = jax.random.fold_in(key, 7919)
    scores = jax.random.randint(mixed, (ELEMS,), 0, 1048576, dtype=jnp.int32)
    scores = scores * ELEMS + jnp.arange(ELEMS, dtype=jnp.int32)
    inverse = jnp.argsort(scores, stable=True).astype(jnp.int32)
    order = jnp.argsort(inverse, stable=True).astype(jnp.int32)
    first = order // 4
    second = order // 2 % 2
    third = order % 2
    offsets = jnp.arange(27, dtype=jnp.int32)
    shift_a = offsets // 9 - 1
    shift_b = offsets // 3 % 3 - 1
    shift_c = offsets % 3 - 1
    span = ELEMS // 4
    near_a = (first[:, None] + shift_a[None, :] + span) % span
    near_b = (second[:, None] + shift_b[None, :] + 2) % 2
    near_c = (third[:, None] + shift_c[None, :] + 2) % 2
    position = near_a * 4 + near_b * 2 + near_c
    return inverse[position].astype(jnp.int32)


def block_levels(rng, shape, cuts, smallest, largest):
    def one(dim, parts):
        draws = jax.random.uniform(jax.random.fold_in(jax.random.fold_in(rng, 6), dim), (parts,), jnp.float32, smallest / len(cuts), largest / len(cuts))
        return jnp.repeat(jnp.exp(draws), shape[dim] // parts).reshape((-1,) + (1,) * (len(shape) - dim - 1))

    gain = one(*cuts[0])
    for cut in cuts[1:]:
        gain = gain * one(*cut)
    return gain


def noise(stream_key, shape, deviation, most, shards=(), kind=jnp.bfloat16):
    factor_of = block_levels(stream_key, shape, shards, -0.22, 0.18) if shards else 1.0
    values = jax.random.normal(stream_key, shape, jnp.float32) * deviation * factor_of
    return jnp.minimum(jnp.maximum(values, -most), most).astype(kind)


def setup_inputs(seed: int = 0) -> dict:
    keys = jax.random.split(jax.random.key(seed), 5)
    return {
        "coefficients": noise(keys[0], (ELEMS, NB, BANDS), 1.0, 6.0, ((0, 2), (2, 16))),
        "hamiltonian": noise(keys[1], (ELEMS, 27, NB, NB), (108 * NB) ** -0.5, 0.0546875, ((0, 2),)),
        "neighbours": draw_neighbours(jax.random.fold_in(keys[4], 71), 0),
        "basis_values": noise(keys[3], (ELEMS, POINTS, NB), NB ** -0.5, 0.5, ((0, 2),)),
    }


def apply_operator(current, hamiltonian, neighbours):
    def one_element(pair):
        block, index = pair
        near = current[index].astype(jnp.float32)
        return jnp.einsum('kij,kjb->ib', block.astype(jnp.float32), near)
    return lax.map(one_element, (hamiltonian, neighbours))


def reference(coefficients, hamiltonian, neighbours, basis_values):
    previous = coefficients.astype(jnp.float32)
    current = apply_operator(coefficients, hamiltonian, neighbours)
    for step in range(CHEB - 1):
        following = 2.0 * apply_operator(current.astype(jnp.bfloat16), hamiltonian, neighbours) - previous
        previous = current
        current = following
    filtered = current.astype(jnp.bfloat16)

    def decode(pair):
        values, coeffs = pair
        orbital = jnp.dot(values, coeffs, preferred_element_type=jnp.float32)
        return jnp.sum(orbital * orbital, axis=1)

    density = lax.map(decode, (basis_values, filtered)) / BANDS
    return filtered, density
```

```python
import functools

import jax
import jax.numpy as jnp
from jax import lax
from jax.experimental import pallas as pl
from jax.experimental.pallas import tpu as pltpu
from jax.sharding import PartitionSpec as P

CHEB = 6
OFFSETS = 27
STEP = 2
MESH = pl.DeviceIdType.MESH


def classes_of(folded):
    groups = {}
    for k in range(OFFSETS):
        shift = (k // 9 - 1, k // 3 % 3 - 1, k % 3 - 1)
        key = tuple(s % 2 if f else s + 1 for s, f in zip(shift, folded))
        groups.setdefault(key, []).append(k)
    return [groups[key] for key in sorted(groups)]


def plain(coefficients, hamiltonian, neighbours, basis_values, bands):
    groups = classes_of((False, True, True))
    wide = hamiltonian.astype(jnp.float32)
    blocks = jnp.stack([sum(wide[:, k] for k in g) for g in groups], axis=1).astype(jnp.bfloat16)
    index = jnp.stack([neighbours[:, g[0]] for g in groups], axis=1)

    def apply_operator(current):
        everyone = lax.all_gather(current, "elem", axis=0, tiled=True)
        return jnp.einsum("ekij,ekjb->eib", blocks, everyone[index], preferred_element_type=jnp.float32)

    previous = coefficients.astype(jnp.float32)
    current = apply_operator(coefficients)
    for _ in range(CHEB - 1):
        following = 2.0 * apply_operator(current.astype(jnp.bfloat16)) - previous
        previous, current = current, following
    filtered = current.astype(jnp.bfloat16)
    orbital = jnp.einsum("epj,ejb->epb", basis_values, filtered, preferred_element_type=jnp.float32)
    terms = jnp.sum(orbital * orbital, axis=2)
    summed = lax.psum_scatter(terms, "band", scatter_dimension=1, tiled=True)
    return filtered, summed / bands


def fused(peers, bands, plane, nb_hbm, c_hbm, h_hbm, b_hbm, f_ref, d_ref,
          hraw, hsum, hd, y0, y1, z0, z1, fsend, fown, frecv, basis, gblock, part, early, rbuf, nb_ref,
          hello, ready, nb_sem, load_sem, c_send, c_recv, h_send, h_recv, f_send, f_recv, d_send, d_recv):
    me = lax.axis_index("elem")
    mine = lax.axis_index("band")
    other = 1 - me
    local, nb, width = c_hbm.shape
    half = width // 2
    elems = 2 * local
    points = b_hbm.shape[1] // peers

    my_rows = pl.ds(me * local, local)
    other_rows = pl.ds(other * local, local)
    my_bands = pl.ds(pl.multiple_of(me * half, half), half)
    other_bands = pl.ds(pl.multiple_of(other * half, half), half)

    loads = [pltpu.make_async_copy(h_hbm.at[e], hraw.at[e], load_sem.at[e]) for e in range(local)]
    loads[0].start()
    nb_load = pltpu.make_async_copy(nb_hbm, nb_ref, nb_sem)
    nb_load.start()
    for copy in loads[1:]:
        copy.start()
    c_load = pltpu.make_async_copy(c_hbm.at[:, :, my_bands], y0.at[my_rows], load_sem.at[local])
    c_load.start()
    b_loads = [pltpu.make_async_copy(b_hbm.at[e], basis.at[e // 2, :, pl.ds(e % 2 * nb, nb)], load_sem.at[local + 1 + e]) for e in range(local)]
    for copy in b_loads:
        copy.start()

    barrier = pltpu.get_barrier_semaphore()

    @pl.when(me == 1)
    def _():
        pl.semaphore_signal(barrier, inc=1, device_id=(0, mine), device_id_type=MESH)

    @pl.when(me == 0)
    def _():
        pl.semaphore_wait(barrier, 1)
        pl.semaphore_signal(hello, inc=1, device_id=(1, mine), device_id_type=MESH)

    @pl.when(me == 1)
    def _():
        pl.semaphore_wait(hello, 1)

    c_copy = pltpu.make_async_remote_copy(
        src_ref=c_hbm.at[:, :, other_bands], dst_ref=y0.at[my_rows],
        send_sem=c_send, recv_sem=c_recv, device_id=(other, mine), device_id_type=MESH)
    c_copy.start()

    @pl.when(me == 1)
    def _():
        for i in range(1, peers):
            pl.semaphore_signal(barrier, inc=1, device_id=(1, lax.rem(mine + i, peers)), device_id_type=MESH)

    groups = classes_of((True, True, True))
    n = len(groups)

    def place(g):
        total = 0
        for c in range(1, n):
            total = total + jnp.where(nb_ref[0, groups[c][0]] == g, c, 0)
        return lax.rem(total, n)

    nb_load.wait()
    spots = [place(g) for g in range(elems)]

    def collapse(e):
        loads[e].wait()
        for c, group in enumerate(groups):
            total = hraw[e, group[0]].astype(jnp.float32)
            for k in group[1:]:
                total = total + hraw[e, k].astype(jnp.float32)
            hsum[e, c] = (total + total).astype(jnp.bfloat16)
        mine_spot = place(me * local + e)
        for g in range(elems):
            hd[me * local + e, :, g * nb:(g + 1) * nb] = hsum[e, mine_spot ^ spots[g]]

    h_copies = []
    for e in range(local):
        collapse(e)
        copy = pltpu.make_async_remote_copy(
            src_ref=hd.at[me * local + e], dst_ref=hd.at[me * local + e],
            send_sem=h_send.at[e], recv_sem=h_recv.at[e], device_id=(other, mine), device_id_type=MESH)
        copy.start()
        h_copies.append(copy)
    c_load.wait()
    c_copy.wait_recv()

    y, z = (y0, y1), (z0, z1)

    def product(source, at, count):
        left = hd[at].reshape(count * nb, elems * nb)
        right = y[source][...].reshape(elems * nb, half)
        out = jnp.dot(left, right, preferred_element_type=jnp.float32)
        return out.reshape(count, nb, half)

    def begin(at, count):
        rows = pl.ds(at, count)
        first = 0.5 * product(0, rows, count)
        z1[rows] = first
        y1[rows] = first.astype(jnp.bfloat16)

    begin(me * local, local)
    for e in range(0, local, STEP):
        for copy in h_copies[e:e + STEP]:
            copy.wait_recv()
        begin(other * local + e, STEP)
    for step in range(1, CHEB - 1):
        now, later = step % 2, (step + 1) % 2
        for which in (slice(0, local), slice(local, elems)):
            before = y0[which].astype(jnp.float32) if step == 1 else z[later][which]
            following = product(now, which, local) - before
            if step < CHEB - 2:
                z[later][which] = following
            y[later][which] = following.astype(jnp.bfloat16)

    now, later = (CHEB - 1) % 2, CHEB % 2
    fsend[...] = (product(now, other_rows, local) - z[later][other_rows]).astype(jnp.bfloat16)
    f_copy = pltpu.make_async_remote_copy(
        src_ref=fsend, dst_ref=frecv, send_sem=f_send, recv_sem=f_recv,
        device_id=(other, mine), device_id_type=MESH)
    f_copy.start()
    fown[...] = (product(now, my_rows, local) - z[later][my_rows]).astype(jnp.bfloat16)
    f_ref[:, :, my_bands] = fown[...]

    def gram(block):
        return lax.dot_general(block, block, (((1,), (1,)), ((), ())), preferred_element_type=jnp.float32)

    grams = [gram(fown[e]) for e in range(local)]
    gblock[...] = jnp.zeros(gblock.shape, gblock.dtype)
    for copy in b_loads:
        copy.wait()
    f_copy.wait_recv()
    f_ref[:, :, other_bands] = frecv[...]
    for e in range(local):
        at = pl.ds(e % 2 * nb, nb)
        gblock[e // 2, at, at] = (grams[e] + gram(frecv[e])).astype(jnp.bfloat16)
    pick = (lax.broadcasted_iota(jnp.int32, (8, 2 * nb), 0)
            == lax.broadcasted_iota(jnp.int32, (8, 2 * nb), 1) // nb).astype(jnp.bfloat16)

    def terms(start, size, store):
        at = pl.ds(start, size)
        for pair in range(local // 2):
            values = basis[pair, at]
            moved = jnp.dot(values, gblock[pair], preferred_element_type=jnp.float32)
            products = moved * values.astype(jnp.float32)
            if pair % 2:
                sums = lax.dot_general(pick, products.astype(jnp.bfloat16), (((1,), (1,)), ((), ())),
                                       preferred_element_type=jnp.float32)
                for column in range(0, size, points):
                    store(column, slice(2 * pair, 2 * pair + 2), slice(0, points), sums[:2, column:column + points])
                continue
            for k in range(2):
                sums = jnp.sum(products[:, k * nb:(k + 1) * nb].reshape(size // 128, 128, nb), axis=2)
                for r in range(size // 128):
                    column = r * 128 // points * points
                    store(column, slice(2 * pair + k, 2 * pair + k + 1),
                          slice(r * 128 - column, r * 128 - column + 128), sums[r:r + 1])

    def group_terms(group):
        def store(column, rows, columns, value):
            part[group * plane + column // points, rows, columns] = value
        terms(pl.multiple_of(group * plane * points, plane * points), plane * points, store)

    def early_terms():
        def store(column, rows, columns, value):
            early[rows, columns] = value
        terms(0, points, store)

    def d_copy(i, source=None):
        target = lax.rem(mine + i, peers)
        return pltpu.make_async_remote_copy(
            src_ref=part.at[target] if source is None else source, dst_ref=rbuf.at[i], send_sem=d_send.at[i], recv_sem=d_recv.at[i],
            device_id=(me, target), device_id_type=MESH)

    @pl.when(me == 1)
    def _():
        pl.semaphore_wait(barrier, peers - 1)
        pl.semaphore_signal(ready, inc=1, device_id=(0, mine), device_id_type=MESH)

    @pl.when(me == 0)
    def _():
        pl.semaphore_wait(ready, 1)

    early_terms()

    @pl.when(mine != 0)
    def _():
        d_copy(peers - mine, early).start()

    planes = peers // plane
    own = mine // plane
    for turn in range(planes):
        up = jnp.where(turn < planes - 1 - own, planes - 1 - turn, turn - (planes - 1 - own))
        down = jnp.where(turn < own, turn, planes - 1 - (turn - own))
        group = own if turn == planes - 1 else jnp.where(2 * own < planes, up, down)
        group_terms(group)
        for d in range(1 if turn == planes - 1 else 0, plane):
            target = group * plane + lax.rem(mine + d, plane)

            @pl.when(target != 0)
            def _(target=target):
                d_copy(lax.rem(target - mine + peers, peers)).start()
    total = part[mine]
    for i in range(1, peers):
        d_copy(i).wait_recv()
        total = total + rbuf[i]
    d_ref[...] = total / bands

    for i in range(1, peers):
        d_copy(i).wait_send()
    c_copy.wait_send()
    for copy in h_copies:
        copy.wait_send()
    f_copy.wait_send()


def deliver(f_in, d_in, f_hbm, d_hbm, sem):
    copies = [pltpu.make_async_copy(f_in, f_hbm, sem.at[0]), pltpu.make_async_copy(d_in, d_hbm, sem.at[1])]
    for copy in copies:
        copy.start()
    for copy in copies:
        copy.wait()


def quick(coefficients, hamiltonian, neighbours, basis_values, peers, bands):
    local, nb, width = coefficients.shape
    half = width // 2
    elems = 2 * local
    points = basis_values.shape[1]
    share = points // peers
    plane = 4 if peers % 4 == 0 else 1
    bf16, f32, dma = jnp.bfloat16, jnp.float32, pltpu.SemaphoreType.DMA
    grant = 67043328 - 2 * local * nb * width - 4 * local * share
    filtered, density = pl.pallas_call(
        functools.partial(fused, peers, bands, plane),
        out_shape=(pltpu.VMEM((local, nb, width), bf16), pltpu.VMEM((local, share), f32)),
        in_specs=[pl.BlockSpec(memory_space=pltpu.HBM)] * 4,
        out_specs=(pl.BlockSpec(memory_space=pltpu.VMEM), pl.BlockSpec(memory_space=pltpu.VMEM)),
        scratch_shapes=[
            pltpu.VMEM((local, OFFSETS, nb, nb), bf16),
            pltpu.VMEM((local, 8, nb, nb), bf16),
            pltpu.VMEM((elems, nb, elems * nb), bf16),
            pltpu.VMEM((elems, nb, half), bf16),
            pltpu.VMEM((elems, nb, half), bf16),
            pltpu.VMEM((elems, nb, half), f32),
            pltpu.VMEM((elems, nb, half), f32),
            pltpu.VMEM((local, nb, half), bf16),
            pltpu.VMEM((local, nb, half), bf16),
            pltpu.VMEM((local, nb, half), bf16),
            pltpu.VMEM((local // 2, points, 2 * nb), bf16),
            pltpu.VMEM((local // 2, 2 * nb, 2 * nb), bf16),
            pltpu.VMEM((peers, local, share), f32),
            pltpu.VMEM((local, share), f32),
            pltpu.VMEM((peers, local, share), f32),
            pltpu.SMEM(neighbours.shape, jnp.int32),
            pltpu.SemaphoreType.REGULAR, pltpu.SemaphoreType.REGULAR,
            dma,
            dma((2 * local + 1,)),
            dma, dma,
            dma((local,)), dma((local,)),
            dma, dma,
            dma((peers,)), dma((peers,)),
        ],
        compiler_params=pltpu.CompilerParams(
            collective_id=0, has_side_effects=True, vmem_limit_bytes=grant),
    )(neighbours, coefficients, hamiltonian, basis_values)
    return pl.pallas_call(
        deliver,
        out_shape=(jax.ShapeDtypeStruct((local, nb, width), bf16), jax.ShapeDtypeStruct((local, share), f32)),
        in_specs=[pl.BlockSpec(memory_space=pltpu.VMEM)] * 2,
        out_specs=(pl.BlockSpec(memory_space=pl.ANY), pl.BlockSpec(memory_space=pl.ANY)),
        scratch_shapes=[dma((2,))],
        compiler_params=pltpu.CompilerParams(vmem_limit_bytes=4 * 2**20),
    )(filtered, density)


def solution(mesh):
    split, peers = mesh.shape["elem"], mesh.shape["band"]

    def local(coefficients, hamiltonian, neighbours, basis_values):
        count, nb, width = coefficients.shape
        bands = width * peers
        fits = (split == 2 and count * split == 8 and nb == 128 and width % 256 == 0
                and basis_values.shape[1] % (128 * peers) == 0)
        if fits:
            return quick(coefficients, hamiltonian, neighbours, basis_values, peers, bands)
        return plain(coefficients, hamiltonian, neighbours, basis_values, bands)

    return jax.shard_map(
        local,
        mesh=mesh,
        in_specs=(
            P("elem", None, "band"),
            P("elem", None, None, None),
            P("elem", None),
            P("elem", None, None),
        ),
        out_specs=(P("elem", None, "band"), P("elem", "band")),
        check_vma=False,
    )
```

```python
import functools

import jax
import jax.numpy as jnp
from jax import lax
from jax.experimental import pallas as pl
from jax.experimental.pallas import tpu as pltpu
from jax.sharding import PartitionSpec as P

CHEB = 6
OFFSETS = 27
STEP = 2
SPLIT = 2
MESH = pl.DeviceIdType.MESH


def classes_of(folded):
    groups = {}
    for k in range(OFFSETS):
        shift = (k // 9 - 1, k // 3 % 3 - 1, k % 3 - 1)
        key = tuple(s % 2 if f else s + 1 for s, f in zip(shift, folded))
        groups.setdefault(key, []).append(k)
    return [groups[key] for key in sorted(groups)]


def chunks_of(local, nb):
    return [(e, at, nb // n) for e in range(local) for n in [SPLIT if e == 0 else 1] for at in range(0, nb, nb // n)]


def plain(coefficients, hamiltonian, neighbours, basis_values, bands):
    groups = classes_of((False, True, True))
    wide = hamiltonian.astype(jnp.float32)
    blocks = jnp.stack([sum(wide[:, k] for k in g) for g in groups], axis=1).astype(jnp.bfloat16)
    index = jnp.stack([neighbours[:, g[0]] for g in groups], axis=1)

    def apply_operator(current):
        everyone = lax.all_gather(current, "elem", axis=0, tiled=True)
        return jnp.einsum("ekij,ekjb->eib", blocks, everyone[index], preferred_element_type=jnp.float32)

    previous = coefficients.astype(jnp.float32)
    current = apply_operator(coefficients)
    for _ in range(CHEB - 1):
        following = 2.0 * apply_operator(current.astype(jnp.bfloat16)) - previous
        previous, current = current, following
    filtered = current.astype(jnp.bfloat16)
    orbital = jnp.einsum("epj,ejb->epb", basis_values, filtered, preferred_element_type=jnp.float32)
    terms = jnp.sum(orbital * orbital, axis=2)
    summed = lax.psum_scatter(terms, "band", scatter_dimension=1, tiled=True)
    return filtered, summed / bands


def fused(peers, bands, plane, nb_hbm, c_hbm, h_hbm, b_hbm, f_ref, d_ref,
          hraw, hsum, hd, y0, y1, z0, z1, fall, frecv, basis, near, gblock, part, early, rbuf, ebuf, nb_ref,
          hello, ready, nb_sem, load_sem, c_send, c_recv, h_load, h_send, h_recv, f_send, f_recv, t_send, t_recv,
          d_send, d_recv, e_send, e_recv):
    me = lax.axis_index("elem")
    mine = lax.axis_index("band")
    other = 1 - me
    local, nb, width = c_hbm.shape
    half = width // 2
    elems = 2 * local
    points = b_hbm.shape[1] // peers

    my_rows = pl.ds(me * local, local)
    other_rows = pl.ds(other * local, local)
    my_bands = pl.ds(pl.multiple_of(me * half, half), half)
    other_bands = pl.ds(pl.multiple_of(other * half, half), half)

    cuts = chunks_of(local, nb)
    loads = [pltpu.make_async_copy(h_hbm.at[e, :, pl.ds(at, rows)], hraw.at[e, :, pl.ds(at, rows)], h_load.at[i])
             for i, (e, at, rows) in enumerate(cuts)]
    loads[0].start()
    nb_load = pltpu.make_async_copy(nb_hbm, nb_ref, nb_sem)
    nb_load.start()
    for copy in loads[1:]:
        copy.start()
    c_load = pltpu.make_async_copy(c_hbm.at[:, :, my_bands], y0.at[my_rows], load_sem.at[local])
    c_load.start()
    b_loads = [pltpu.make_async_copy(b_hbm.at[e], basis.at[e // 2, :, pl.ds(e % 2 * nb, nb)], load_sem.at[local + 1 + e]) for e in range(local)]

    barrier = pltpu.get_barrier_semaphore()

    @pl.when(me == 1)
    def _():
        pl.semaphore_signal(barrier, inc=1, device_id=(0, mine), device_id_type=MESH)

    @pl.when(me == 0)
    def _():
        pl.semaphore_wait(barrier, 1)
        pl.semaphore_signal(hello, inc=1, device_id=(1, mine), device_id_type=MESH)

    @pl.when(me == 1)
    def _():
        pl.semaphore_wait(hello, 1)

    c_copy = pltpu.make_async_remote_copy(
        src_ref=c_hbm.at[:, :, other_bands], dst_ref=y0.at[my_rows],
        send_sem=c_send, recv_sem=c_recv, device_id=(other, mine), device_id_type=MESH)
    c_copy.start()

    @pl.when(me == 1)
    def _():
        for i in range(1, peers):
            pl.semaphore_signal(barrier, inc=1, device_id=(1, lax.rem(mine + i, peers)), device_id_type=MESH)

    groups = classes_of((True, True, True))
    n = len(groups)

    def place(g):
        total = 0
        for c in range(1, n):
            total = total + jnp.where(nb_ref[0, groups[c][0]] == g, c, 0)
        return lax.rem(total, n)

    nb_load.wait()
    spots = [place(g) for g in range(elems)]

    def collapse(i, e, at, rows):
        loads[i].wait()
        here = slice(at, at + rows)
        for c, group in enumerate(groups):
            total = hraw[e, group[0], here].astype(jnp.float32)
            for k in group[1:]:
                total = total + hraw[e, k, here].astype(jnp.float32)
            hsum[e, c, here] = (total + total).astype(jnp.bfloat16)
        mine_spot = place(me * local + e)
        for g in range(elems):
            hd[me * local + e, here, g * nb:(g + 1) * nb] = hsum[e, mine_spot ^ spots[g], here]

    h_copies = []
    for i, (e, at, rows) in enumerate(cuts):
        collapse(i, e, at, rows)
        copy = pltpu.make_async_remote_copy(
            src_ref=hd.at[me * local + e, pl.ds(at, rows)], dst_ref=hd.at[me * local + e, pl.ds(at, rows)],
            send_sem=h_send.at[i], recv_sem=h_recv.at[i], device_id=(other, mine), device_id_type=MESH)
        copy.start()
        h_copies.append(copy)
    for copy in b_loads:
        copy.start()
    t_copy = pltpu.make_async_remote_copy(
        src_ref=b_hbm.at[:, pl.ds(0, points)], dst_ref=near.at[my_rows],
        send_sem=t_send, recv_sem=t_recv, device_id=(other, mine), device_id_type=MESH)
    t_copy.start()
    n_load = pltpu.make_async_copy(b_hbm.at[:, pl.ds(0, points)], near.at[my_rows], load_sem.at[2 * local + 1])
    n_load.start()
    c_load.wait()
    c_copy.wait_recv()

    y, z = (y0, y1), (z0, z1)

    def product(source, at, count):
        left = hd[at].reshape(count * nb, elems * nb)
        right = y[source][...].reshape(elems * nb, half)
        out = jnp.dot(left, right, preferred_element_type=jnp.float32)
        return out.reshape(count, nb, half)

    def begin(at, count):
        rows = pl.ds(at, count)
        first = 0.5 * product(0, rows, count)
        z1[rows] = first
        y1[rows] = first.astype(jnp.bfloat16)

    begin(me * local, local)
    for e in range(0, local, STEP):
        for copy, cut in zip(h_copies, cuts):
            if e <= cut[0] < e + STEP:
                copy.wait_recv()
        begin(other * local + e, STEP)
    for step in range(1, CHEB - 1):
        now, later = step % 2, (step + 1) % 2
        for which in (slice(0, local), slice(local, elems)):
            before = y0[which].astype(jnp.float32) if step == 1 else z[later][which]
            following = product(now, which, local) - before
            if step < CHEB - 2:
                z[later][which] = following
            y[later][which] = following.astype(jnp.bfloat16)

    def early_terms(side):
        for e in range(local):
            orbital = jnp.dot(near[side * local + e], fall[side * local + e], preferred_element_type=jnp.float32)
            squares = sum(orbital[:, at:at + 128] * orbital[:, at:at + 128] for at in range(0, half, 128))
            sums = jnp.sum(squares.reshape(points // 128, 128, 128), axis=2)
            for r in range(points // 128):
                early[side, e:e + 1, r * 128:(r + 1) * 128] = sums[r:r + 1]

    def e_copy(side):
        slot = lax.rem(me + side, 2) * peers + mine
        copy = pltpu.make_async_remote_copy(
            src_ref=early.at[side], dst_ref=ebuf.at[slot], send_sem=e_send.at[side], recv_sem=e_recv,
            device_id=(side, 0), device_id_type=MESH)
        return slot != 0, copy

    @pl.when(me == 1)
    def _():
        pl.semaphore_wait(barrier, peers - 1)
        pl.semaphore_signal(ready, inc=1, device_id=(0, mine), device_id_type=MESH)

    @pl.when(me == 0)
    def _():
        pl.semaphore_wait(ready, 1)

    t_copy.wait_recv()
    n_load.wait()
    now, later = (CHEB - 1) % 2, CHEB % 2
    f_copy = pltpu.make_async_remote_copy(
        src_ref=fall.at[other_rows], dst_ref=frecv, send_sem=f_send, recv_sem=f_recv,
        device_id=(other, mine), device_id_type=MESH)
    for side in range(2):
        which = slice(side * local, (side + 1) * local)
        fall[which] = (product(now, which, local) - z[later][which]).astype(jnp.bfloat16)

        @pl.when(me != side)
        def _():
            f_copy.start()

        early_terms(side)
        sends, copy = e_copy(side)

        @pl.when(sends)
        def _(copy=copy):
            copy.start()

    f_ref[:, :, my_bands] = fall[my_rows]

    def gram(block):
        return lax.dot_general(block, block, (((1,), (1,)), ((), ())), preferred_element_type=jnp.float32)

    for copy in b_loads:
        copy.wait()
    grams = [gram(fall[me * local + e]) for e in range(local)]
    gblock[...] = jnp.zeros(gblock.shape, gblock.dtype)
    pick = (lax.broadcasted_iota(jnp.int32, (8, 2 * nb), 0)
            == lax.broadcasted_iota(jnp.int32, (8, 2 * nb), 1) // nb).astype(jnp.bfloat16)

    def terms(values, block, pair, store):
        size = values.shape[0]
        moved = jnp.dot(values, block, preferred_element_type=jnp.float32)
        products = moved * values.astype(jnp.float32)
        if pair % 2:
            sums = lax.dot_general(pick, products.astype(jnp.bfloat16), (((1,), (1,)), ((), ())),
                                   preferred_element_type=jnp.float32)
            for column in range(0, size, points):
                store(column, slice(2 * pair, 2 * pair + 2), slice(0, points), sums[:2, column:column + points])
            return
        for k in range(2):
            sums = jnp.sum(products[:, k * nb:(k + 1) * nb].reshape(size // 128, 128, nb), axis=2)
            for r in range(size // 128):
                column = r * 128 // points * points
                store(column, slice(2 * pair + k, 2 * pair + k + 1),
                      slice(r * 128 - column, r * 128 - column + 128), sums[r:r + 1])

    def group_terms(group):
        size = plane * points
        at = pl.ds(pl.multiple_of(group * size, size), size)

        def store(column, rows, columns, value):
            part[group * plane + column // points, rows, columns] = value
        for pair in range(local // 2):
            terms(basis[pair, at], gblock[pair], pair, store)

    def d_copy(i):
        target = lax.rem(mine + i, peers)
        return pltpu.make_async_remote_copy(
            src_ref=part.at[target], dst_ref=rbuf.at[i], send_sem=d_send.at[i], recv_sem=d_recv.at[i],
            device_id=(me, target), device_id_type=MESH)

    f_copy.wait_recv()
    f_ref[:, :, other_bands] = frecv[...]
    for e in range(local):
        at = pl.ds(e % 2 * nb, nb)
        gblock[e // 2, at, at] = (grams[e] + gram(frecv[e])).astype(jnp.bfloat16)

    planes = peers // plane
    own = mine // plane
    for turn in range(planes):
        up = jnp.where(turn < planes - 1 - own, planes - 1 - turn, turn - (planes - 1 - own))
        down = jnp.where(turn < own, turn, planes - 1 - (turn - own))
        group = own if turn == planes - 1 else jnp.where(2 * own < planes, up, down)
        group_terms(group)
        for d in range(1 if turn == planes - 1 else 0, plane):
            target = group * plane + lax.rem(mine + d, plane)

            @pl.when(target != 0)
            def _(target=target):
                d_copy(lax.rem(target - mine + peers, peers)).start()
    @pl.when(mine == 0)
    def _():
        arrived = ebuf.at[pl.ds(1, 2 * peers - 1)]
        pltpu.make_async_copy(arrived, arrived, e_recv).wait()
        total = early[me]
        for i in range(1, 2 * peers):
            total = total + ebuf[i]
        d_ref[...] = total / bands

    @pl.when(mine != 0)
    def _():
        total = part[mine]
        for i in range(1, peers):
            d_copy(i).wait_recv()
            total = total + rbuf[i]
        d_ref[...] = total / bands

    for side in range(2):
        sends, copy = e_copy(side)

        @pl.when(sends)
        def _(copy=copy):
            copy.wait_send()
    for i in range(1, peers):
        @pl.when(lax.rem(mine + i, peers) != 0)
        def _(i=i):
            d_copy(i).wait_send()
    t_copy.wait_send()
    c_copy.wait_send()
    for copy in h_copies:
        copy.wait_send()
    f_copy.wait_send()


def deliver(f_in, d_in, f_hbm, d_hbm, sem):
    copies = [pltpu.make_async_copy(f_in, f_hbm, sem.at[0]), pltpu.make_async_copy(d_in, d_hbm, sem.at[1])]
    for copy in copies:
        copy.start()
    for copy in copies:
        copy.wait()


def quick(coefficients, hamiltonian, neighbours, basis_values, peers, bands):
    local, nb, width = coefficients.shape
    half = width // 2
    elems = 2 * local
    points = basis_values.shape[1]
    share = points // peers
    plane = 4 if peers % 4 == 0 else 1
    bf16, f32, dma = jnp.bfloat16, jnp.float32, pltpu.SemaphoreType.DMA
    grant = 67043328 - 2 * local * nb * width - 4 * local * share
    filtered, density = pl.pallas_call(
        functools.partial(fused, peers, bands, plane),
        out_shape=(pltpu.VMEM((local, nb, width), bf16), pltpu.VMEM((local, share), f32)),
        in_specs=[pl.BlockSpec(memory_space=pltpu.HBM)] * 4,
        out_specs=(pl.BlockSpec(memory_space=pltpu.VMEM), pl.BlockSpec(memory_space=pltpu.VMEM)),
        scratch_shapes=[
            pltpu.VMEM((local, OFFSETS, nb, nb), bf16),
            pltpu.VMEM((local, 8, nb, nb), bf16),
            pltpu.VMEM((elems, nb, elems * nb), bf16),
            pltpu.VMEM((elems, nb, half), bf16),
            pltpu.VMEM((elems, nb, half), bf16),
            pltpu.VMEM((elems, nb, half), f32),
            pltpu.VMEM((elems, nb, half), f32),
            pltpu.VMEM((elems, nb, half), bf16),
            pltpu.VMEM((local, nb, half), bf16),
            pltpu.VMEM((local // 2, points, 2 * nb), bf16),
            pltpu.VMEM((elems, share, nb), bf16),
            pltpu.VMEM((local // 2, 2 * nb, 2 * nb), bf16),
            pltpu.VMEM((peers, local, share), f32),
            pltpu.VMEM((2, local, share), f32),
            pltpu.VMEM((peers, local, share), f32),
            pltpu.VMEM((2 * peers, local, share), f32),
            pltpu.SMEM(neighbours.shape, jnp.int32),
            pltpu.SemaphoreType.REGULAR, pltpu.SemaphoreType.REGULAR,
            dma,
            dma((2 * local + 2,)),
            dma, dma,
            dma((len(chunks_of(local, nb)),)), dma((len(chunks_of(local, nb)),)), dma((len(chunks_of(local, nb)),)),
            dma, dma,
            dma, dma,
            dma((peers,)), dma((peers,)),
            dma((2,)), dma,
        ],
        compiler_params=pltpu.CompilerParams(
            collective_id=0, has_side_effects=True, vmem_limit_bytes=grant),
    )(neighbours, coefficients, hamiltonian, basis_values)
    return pl.pallas_call(
        deliver,
        out_shape=(jax.ShapeDtypeStruct((local, nb, width), bf16), jax.ShapeDtypeStruct((local, share), f32)),
        in_specs=[pl.BlockSpec(memory_space=pltpu.VMEM)] * 2,
        out_specs=(pl.BlockSpec(memory_space=pl.ANY), pl.BlockSpec(memory_space=pl.ANY)),
        scratch_shapes=[dma((2,))],
        compiler_params=pltpu.CompilerParams(vmem_limit_bytes=4 * 2**20),
    )(filtered, density)


def solution(mesh):
    split, peers = mesh.shape["elem"], mesh.shape["band"]

    def local(coefficients, hamiltonian, neighbours, basis_values):
        count, nb, width = coefficients.shape
        bands = width * peers
        fits = (split == 2 and count * split == 8 and nb == 128 and width % 256 == 0
                and basis_values.shape[1] % (128 * peers) == 0)
        if fits:
            return quick(coefficients, hamiltonian, neighbours, basis_values, peers, bands)
        return plain(coefficients, hamiltonian, neighbours, basis_values, bands)

    return jax.shard_map(
        local,
        mesh=mesh,
        in_specs=(
            P("elem", None, "band"),
            P("elem", None, None, None),
            P("elem", None),
            P("elem", None, None),
        ),
        out_specs=(P("elem", None, "band"), P("elem", "band")),
        check_vma=False,
    )
```

```python
import functools

import jax
import jax.numpy as jnp
from jax import lax
from jax.experimental import pallas as pl
from jax.experimental.pallas import tpu as pltpu
from jax.sharding import PartitionSpec as P

CHEB = 6
OFFSETS = 27
STEP = 2
SPLIT = 2
MESH = pl.DeviceIdType.MESH


def classes_of(folded):
    groups = {}
    for k in range(OFFSETS):
        shift = (k // 9 - 1, k // 3 % 3 - 1, k % 3 - 1)
        key = tuple(s % 2 if f else s + 1 for s, f in zip(shift, folded))
        groups.setdefault(key, []).append(k)
    return [groups[key] for key in sorted(groups)]


def chunks_of(local, nb):
    return [(e, at, nb // n) for e in range(local) for n in [SPLIT if e == 0 else 1] for at in range(0, nb, nb // n)]


def plain(coefficients, hamiltonian, neighbours, basis_values, bands):
    groups = classes_of((False, True, True))
    wide = hamiltonian.astype(jnp.float32)
    blocks = jnp.stack([sum(wide[:, k] for k in g) for g in groups], axis=1).astype(jnp.bfloat16)
    index = jnp.stack([neighbours[:, g[0]] for g in groups], axis=1)

    def apply_operator(current):
        everyone = lax.all_gather(current, "elem", axis=0, tiled=True)
        return jnp.einsum("ekij,ekjb->eib", blocks, everyone[index], preferred_element_type=jnp.float32)

    previous = coefficients.astype(jnp.float32)
    current = apply_operator(coefficients)
    for _ in range(CHEB - 1):
        following = 2.0 * apply_operator(current.astype(jnp.bfloat16)) - previous
        previous, current = current, following
    filtered = current.astype(jnp.bfloat16)
    orbital = jnp.einsum("epj,ejb->epb", basis_values, filtered, preferred_element_type=jnp.float32)
    terms = jnp.sum(orbital * orbital, axis=2)
    summed = lax.psum_scatter(terms, "band", scatter_dimension=1, tiled=True)
    return filtered, summed / bands


def fused(peers, bands, plane, nb_hbm, c_hbm, h_hbm, b_hbm, f_ref, d_ref,
          hraw, hsum, hd, y0, y1, z0, z1, fall, frecv, basis, near, gblock, part, early, ahead, rbuf, ebuf, nb_ref,
          hello, ready, nb_sem, load_sem, c_send, c_recv, h_load, h_send, h_recv, f_send, f_recv, t_send, t_recv,
          d_send, d_recv, e_send, e_recv):
    me = lax.axis_index("elem")
    mine = lax.axis_index("band")
    other = 1 - me
    local, nb, width = c_hbm.shape
    half = width // 2
    elems = 2 * local
    points = b_hbm.shape[1] // peers

    my_rows = pl.ds(me * local, local)
    other_rows = pl.ds(other * local, local)
    my_bands = pl.ds(pl.multiple_of(me * half, half), half)
    other_bands = pl.ds(pl.multiple_of(other * half, half), half)

    cuts = chunks_of(local, nb)
    loads = [pltpu.make_async_copy(h_hbm.at[e, :, pl.ds(at, rows)], hraw.at[e, :, pl.ds(at, rows)], h_load.at[i])
             for i, (e, at, rows) in enumerate(cuts)]
    loads[0].start()
    nb_load = pltpu.make_async_copy(nb_hbm, nb_ref, nb_sem)
    nb_load.start()
    for copy in loads[1:]:
        copy.start()
    c_load = pltpu.make_async_copy(c_hbm.at[:, :, my_bands], y0.at[my_rows], load_sem.at[local])
    c_load.start()
    b_loads = [pltpu.make_async_copy(b_hbm.at[e], basis.at[e // 2, :, pl.ds(e % 2 * nb, nb)], load_sem.at[local + 1 + e]) for e in range(local)]

    barrier = pltpu.get_barrier_semaphore()

    @pl.when(me == 1)
    def _():
        pl.semaphore_signal(barrier, inc=1, device_id=(0, mine), device_id_type=MESH)

    @pl.when(me == 0)
    def _():
        pl.semaphore_wait(barrier, 1)
        pl.semaphore_signal(hello, inc=1, device_id=(1, mine), device_id_type=MESH)

    @pl.when(me == 1)
    def _():
        pl.semaphore_wait(hello, 1)

    c_copy = pltpu.make_async_remote_copy(
        src_ref=c_hbm.at[:, :, other_bands], dst_ref=y0.at[my_rows],
        send_sem=c_send, recv_sem=c_recv, device_id=(other, mine), device_id_type=MESH)
    c_copy.start()

    @pl.when(me == 1)
    def _():
        for i in range(1, peers):
            pl.semaphore_signal(barrier, inc=1, device_id=(1, lax.rem(mine + i, peers)), device_id_type=MESH)

    groups = classes_of((True, True, True))
    n = len(groups)

    def place(g):
        total = 0
        for c in range(1, n):
            total = total + jnp.where(nb_ref[0, groups[c][0]] == g, c, 0)
        return lax.rem(total, n)

    nb_load.wait()
    spots = [place(g) for g in range(elems)]

    def collapse(i, e, at, rows):
        loads[i].wait()
        here = slice(at, at + rows)
        for c, group in enumerate(groups):
            total = hraw[e, group[0], here].astype(jnp.float32)
            for k in group[1:]:
                total = total + hraw[e, k, here].astype(jnp.float32)
            hsum[e, c, here] = (total + total).astype(jnp.bfloat16)
        mine_spot = place(me * local + e)
        for g in range(elems):
            hd[me * local + e, here, g * nb:(g + 1) * nb] = hsum[e, mine_spot ^ spots[g], here]

    h_copies = []
    for i, (e, at, rows) in enumerate(cuts):
        collapse(i, e, at, rows)
        copy = pltpu.make_async_remote_copy(
            src_ref=hd.at[me * local + e, pl.ds(at, rows)], dst_ref=hd.at[me * local + e, pl.ds(at, rows)],
            send_sem=h_send.at[i], recv_sem=h_recv.at[i], device_id=(other, mine), device_id_type=MESH)
        copy.start()
        h_copies.append(copy)
    for copy in b_loads:
        copy.start()
    t_copy = pltpu.make_async_remote_copy(
        src_ref=b_hbm.at[:, pl.ds(0, points)], dst_ref=near,
        send_sem=t_send, recv_sem=t_recv, device_id=(1, mine), device_id_type=MESH)
    n_load = pltpu.make_async_copy(b_hbm.at[:, pl.ds(0, points)], near, load_sem.at[2 * local + 1])

    @pl.when(me == 0)
    def _():
        t_copy.start()
        n_load.start()

    c_load.wait()
    c_copy.wait_recv()

    y, z = (y0, y1), (z0, z1)

    def product(source, at, count):
        left = hd[at].reshape(count * nb, elems * nb)
        right = y[source][...].reshape(elems * nb, half)
        out = jnp.dot(left, right, preferred_element_type=jnp.float32)
        return out.reshape(count, nb, half)

    def begin(at, count):
        rows = pl.ds(at, count)
        first = 0.5 * product(0, rows, count)
        z1[rows] = first
        y1[rows] = first.astype(jnp.bfloat16)

    begin(me * local, local)
    for e in range(0, local, STEP):
        for copy, cut in zip(h_copies, cuts):
            if e <= cut[0] < e + STEP:
                copy.wait_recv()
        begin(other * local + e, STEP)
    for step in range(1, CHEB - 1):
        now, later = step % 2, (step + 1) % 2
        for which in (slice(0, local), slice(local, elems)):
            before = y0[which].astype(jnp.float32) if step == 1 else z[later][which]
            following = product(now, which, local) - before
            if step < CHEB - 2:
                z[later][which] = following
            y[later][which] = following.astype(jnp.bfloat16)

    def early_terms():
        for e in range(local):
            orbital = jnp.dot(near[e], fall[e], preferred_element_type=jnp.float32)
            squares = sum(orbital[:, at:at + 128] * orbital[:, at:at + 128] for at in range(0, half, 128))
            sums = jnp.sum(squares.reshape(points // 128, 128, 128), axis=2)
            for r in range(points // 128):
                early[e:e + 1, r * 128:(r + 1) * 128] = sums[r:r + 1]

    e_slot = me * peers + mine
    e_copy = pltpu.make_async_remote_copy(
        src_ref=early, dst_ref=ebuf.at[e_slot], send_sem=e_send, recv_sem=e_recv,
        device_id=(0, 0), device_id_type=MESH)

    @pl.when(me == 0)
    def _():
        n_load.wait()

    @pl.when(me == 1)
    def _():
        t_copy.wait_recv()

    now, later = (CHEB - 1) % 2, CHEB % 2
    f_copy = pltpu.make_async_remote_copy(
        src_ref=fall.at[other_rows], dst_ref=frecv, send_sem=f_send, recv_sem=f_recv,
        device_id=(other, mine), device_id_type=MESH)
    def last_step(rows):
        fall[rows] = (product(now, rows, local) - z[later][rows]).astype(jnp.bfloat16)

    last_step(other_rows)
    f_copy.start()

    @pl.when(me == 1)
    def _():
        early_terms()
        pl.semaphore_wait(barrier, peers - 1)
        pl.semaphore_signal(ready, inc=1, device_id=(0, mine), device_id_type=MESH)
        e_copy.start()

    last_step(my_rows)

    @pl.when(me == 0)
    def _():
        early_terms()
        pl.semaphore_wait(ready, 1)

        @pl.when(mine != 0)
        def _():
            e_copy.start()

    f_ref[:, :, my_bands] = fall[my_rows]

    def gram(block):
        return lax.dot_general(block, block, (((1,), (1,)), ((), ())), preferred_element_type=jnp.float32)

    for copy in b_loads:
        copy.wait()
    grams = [gram(fall[me * local + e]) for e in range(local)]
    gblock[...] = jnp.zeros(gblock.shape, gblock.dtype)
    pick = (lax.broadcasted_iota(jnp.int32, (8, 2 * nb), 0)
            == lax.broadcasted_iota(jnp.int32, (8, 2 * nb), 1) // nb).astype(jnp.bfloat16)

    def terms(values, block, pair, store):
        size = values.shape[0]
        moved = jnp.dot(values, block, preferred_element_type=jnp.float32)
        products = moved * values.astype(jnp.float32)
        if pair % 2:
            sums = lax.dot_general(pick, products.astype(jnp.bfloat16), (((1,), (1,)), ((), ())),
                                   preferred_element_type=jnp.float32)
            for column in range(0, size, points):
                store(column, slice(2 * pair, 2 * pair + 2), slice(0, points), sums[:2, column:column + points])
            return
        for k in range(2):
            sums = jnp.sum(products[:, k * nb:(k + 1) * nb].reshape(size // 128, 128, nb), axis=2)
            for r in range(size // 128):
                column = r * 128 // points * points
                store(column, slice(2 * pair + k, 2 * pair + k + 1),
                      slice(r * 128 - column, r * 128 - column + 128), sums[r:r + 1])

    def first_terms():
        def store(column, rows, columns, value):
            ahead[rows, columns] = value
        for pair in range(local // 2):
            terms(basis[pair, pl.ds(0, points)], gblock[pair], pair, store)

    def group_terms(group):
        size = plane * points
        at = pl.ds(pl.multiple_of(group * size, size), size)

        def store(column, rows, columns, value):
            part[group * plane + column // points, rows, columns] = value
        for pair in range(local // 2):
            terms(basis[pair, at], gblock[pair], pair, store)

    def d_copy(i, source=None):
        target = lax.rem(mine + i, peers)
        return pltpu.make_async_remote_copy(
            src_ref=part.at[target] if source is None else source, dst_ref=rbuf.at[i], send_sem=d_send.at[i], recv_sem=d_recv.at[i],
            device_id=(me, target), device_id_type=MESH)

    f_copy.wait_recv()
    f_ref[:, :, other_bands] = frecv[...]
    for e in range(local):
        at = pl.ds(e % 2 * nb, nb)
        gblock[e // 2, at, at] = (grams[e] + gram(frecv[e])).astype(jnp.bfloat16)

    @pl.when(me == 1)
    def _():
        first_terms()

        @pl.when(mine != 0)
        def _():
            d_copy(peers - mine, ahead).start()

    planes = peers // plane
    own = mine // plane
    for turn in range(planes):
        up = jnp.where(turn < planes - 1 - own, planes - 1 - turn, turn - (planes - 1 - own))
        down = jnp.where(turn < own, turn, planes - 1 - (turn - own))
        group = own if turn == planes - 1 else jnp.where(2 * own < planes, up, down)
        group_terms(group)
        for d in range(1 if turn == planes - 1 else 0, plane):
            target = group * plane + lax.rem(mine + d, plane)

            @pl.when(target != 0)
            def _(target=target):
                d_copy(lax.rem(target - mine + peers, peers)).start()
    @pl.when(e_slot == 0)
    def _():
        arrived = ebuf.at[pl.ds(1, 2 * peers - 1)]
        pltpu.make_async_copy(arrived, arrived, e_recv).wait()
        total = early[...]
        for i in range(1, 2 * peers):
            total = total + ebuf[i]
        d_ref[...] = total / bands

    @pl.when(e_slot != 0)
    def _():
        total = part[mine]
        for i in range(1, peers):
            d_copy(i).wait_recv()
            total = total + rbuf[i]
        d_ref[...] = total / bands
        e_copy.wait_send()

    for i in range(1, peers):
        @pl.when(lax.rem(mine + i, peers) + me != 0)
        def _(i=i):
            d_copy(i).wait_send()

    @pl.when(me == 0)
    def _():
        t_copy.wait_send()

    c_copy.wait_send()
    for copy in h_copies:
        copy.wait_send()
    f_copy.wait_send()


def deliver(f_in, d_in, f_hbm, d_hbm, sem):
    copies = [pltpu.make_async_copy(f_in, f_hbm, sem.at[0]), pltpu.make_async_copy(d_in, d_hbm, sem.at[1])]
    for copy in copies:
        copy.start()
    for copy in copies:
        copy.wait()


def quick(coefficients, hamiltonian, neighbours, basis_values, peers, bands):
    local, nb, width = coefficients.shape
    half = width // 2
    elems = 2 * local
    points = basis_values.shape[1]
    share = points // peers
    plane = 4 if peers % 4 == 0 else 1
    bf16, f32, dma = jnp.bfloat16, jnp.float32, pltpu.SemaphoreType.DMA
    grant = 67043328 - 2 * local * nb * width - 4 * local * share
    filtered, density = pl.pallas_call(
        functools.partial(fused, peers, bands, plane),
        out_shape=(pltpu.VMEM((local, nb, width), bf16), pltpu.VMEM((local, share), f32)),
        in_specs=[pl.BlockSpec(memory_space=pltpu.HBM)] * 4,
        out_specs=(pl.BlockSpec(memory_space=pltpu.VMEM), pl.BlockSpec(memory_space=pltpu.VMEM)),
        scratch_shapes=[
            pltpu.VMEM((local, OFFSETS, nb, nb), bf16),
            pltpu.VMEM((local, 8, nb, nb), bf16),
            pltpu.VMEM((elems, nb, elems * nb), bf16),
            pltpu.VMEM((elems, nb, half), bf16),
            pltpu.VMEM((elems, nb, half), bf16),
            pltpu.VMEM((elems, nb, half), f32),
            pltpu.VMEM((elems, nb, half), f32),
            pltpu.VMEM((elems, nb, half), bf16),
            pltpu.VMEM((local, nb, half), bf16),
            pltpu.VMEM((local // 2, points, 2 * nb), bf16),
            pltpu.VMEM((local, share, nb), bf16),
            pltpu.VMEM((local // 2, 2 * nb, 2 * nb), bf16),
            pltpu.VMEM((peers, local, share), f32),
            pltpu.VMEM((local, share), f32),
            pltpu.VMEM((local, share), f32),
            pltpu.VMEM((peers, local, share), f32),
            pltpu.VMEM((2 * peers, local, share), f32),
            pltpu.SMEM(neighbours.shape, jnp.int32),
            pltpu.SemaphoreType.REGULAR, pltpu.SemaphoreType.REGULAR,
            dma,
            dma((2 * local + 2,)),
            dma, dma,
            dma((len(chunks_of(local, nb)),)), dma((len(chunks_of(local, nb)),)), dma((len(chunks_of(local, nb)),)),
            dma, dma,
            dma, dma,
            dma((peers,)), dma((peers,)),
            dma, dma,
        ],
        compiler_params=pltpu.CompilerParams(
            collective_id=0, has_side_effects=True, vmem_limit_bytes=grant),
    )(neighbours, coefficients, hamiltonian, basis_values)
    return pl.pallas_call(
        deliver,
        out_shape=(jax.ShapeDtypeStruct((local, nb, width), bf16), jax.ShapeDtypeStruct((local, share), f32)),
        in_specs=[pl.BlockSpec(memory_space=pltpu.VMEM)] * 2,
        out_specs=(pl.BlockSpec(memory_space=pl.ANY), pl.BlockSpec(memory_space=pl.ANY)),
        scratch_shapes=[dma((2,))],
        compiler_params=pltpu.CompilerParams(vmem_limit_bytes=4 * 2**20),
    )(filtered, density)


def solution(mesh):
    split, peers = mesh.shape["elem"], mesh.shape["band"]

    def local(coefficients, hamiltonian, neighbours, basis_values):
        count, nb, width = coefficients.shape
        bands = width * peers
        fits = (split == 2 and count * split == 8 and nb == 128 and width % 256 == 0
                and basis_values.shape[1] % (128 * peers) == 0)
        if fits:
            return quick(coefficients, hamiltonian, neighbours, basis_values, peers, bands)
        return plain(coefficients, hamiltonian, neighbours, basis_values, bands)

    return jax.shard_map(
        local,
        mesh=mesh,
        in_specs=(
            P("elem", None, "band"),
            P("elem", None, None, None),
            P("elem", None),
            P("elem", None, None),
        ),
        out_specs=(P("elem", None, "band"), P("elem", "band")),
        check_vma=False,
    )
```

```python
import functools

import jax
import jax.numpy as jnp
from jax import lax
from jax.experimental import pallas as pl
from jax.experimental.pallas import tpu as pltpu
from jax.sharding import PartitionSpec as P

CHEB = 6
OFFSETS = 27
STEP = 1
SPLIT = 2
MESH = pl.DeviceIdType.MESH


def classes_of(folded):
    groups = {}
    for k in range(OFFSETS):
        shift = (k // 9 - 1, k // 3 % 3 - 1, k % 3 - 1)
        key = tuple(s % 2 if f else s + 1 for s, f in zip(shift, folded))
        groups.setdefault(key, []).append(k)
    return [groups[key] for key in sorted(groups)]


def chunks_of(local, nb):
    return [(e, at, nb // n) for e in range(local) for n in [SPLIT if e == 0 else 1] for at in range(0, nb, nb // n)]


def plain(coefficients, hamiltonian, neighbours, basis_values, bands):
    groups = classes_of((False, True, True))
    wide = hamiltonian.astype(jnp.float32)
    blocks = jnp.stack([sum(wide[:, k] for k in g) for g in groups], axis=1).astype(jnp.bfloat16)
    index = jnp.stack([neighbours[:, g[0]] for g in groups], axis=1)

    def apply_operator(current):
        everyone = lax.all_gather(current, "elem", axis=0, tiled=True)
        return jnp.einsum("ekij,ekjb->eib", blocks, everyone[index], preferred_element_type=jnp.float32)

    previous = coefficients.astype(jnp.float32)
    current = apply_operator(coefficients)
    for _ in range(CHEB - 1):
        following = 2.0 * apply_operator(current.astype(jnp.bfloat16)) - previous
        previous, current = current, following
    filtered = current.astype(jnp.bfloat16)
    orbital = jnp.einsum("epj,ejb->epb", basis_values, filtered, preferred_element_type=jnp.float32)
    terms = jnp.sum(orbital * orbital, axis=2)
    summed = lax.psum_scatter(terms, "band", scatter_dimension=1, tiled=True)
    return filtered, summed / bands


def fused(peers, bands, plane, nb_hbm, c_hbm, h_hbm, b_hbm, f_ref, d_ref,
          hraw, hsum, hd, y0, y1, z0, z1, fall, frecv, basis, near, gblock, part, early, ahead, rbuf, ebuf, nb_ref,
          hello, ready, nb_sem, load_sem, c_send, c_recv, h_load, h_send, h_recv, f_send, f_recv, t_send, t_recv,
          d_send, d_recv, e_send, e_recv):
    me = lax.axis_index("elem")
    mine = lax.axis_index("band")
    other = 1 - me
    local, nb, width = c_hbm.shape
    half = width // 2
    elems = 2 * local
    points = b_hbm.shape[1] // peers

    my_rows = pl.ds(me * local, local)
    other_rows = pl.ds(other * local, local)
    my_bands = pl.ds(pl.multiple_of(me * half, half), half)
    other_bands = pl.ds(pl.multiple_of(other * half, half), half)

    cuts = chunks_of(local, nb)
    loads = [pltpu.make_async_copy(h_hbm.at[e, :, pl.ds(at, rows)], hraw.at[e, :, pl.ds(at, rows)], h_load.at[i])
             for i, (e, at, rows) in enumerate(cuts)]
    loads[0].start()
    nb_load = pltpu.make_async_copy(nb_hbm, nb_ref, nb_sem)
    nb_load.start()
    for copy in loads[1:]:
        copy.start()
    c_load = pltpu.make_async_copy(c_hbm.at[:, :, my_bands], y0.at[my_rows], load_sem.at[local])
    c_load.start()
    b_loads = [pltpu.make_async_copy(b_hbm.at[e], basis.at[e // 2, :, pl.ds(e % 2 * nb, nb)], load_sem.at[local + 1 + e]) for e in range(local)]

    barrier = pltpu.get_barrier_semaphore()

    @pl.when(me == 1)
    def _():
        pl.semaphore_signal(barrier, inc=1, device_id=(0, mine), device_id_type=MESH)

    @pl.when(me == 0)
    def _():
        pl.semaphore_wait(barrier, 1)
        pl.semaphore_signal(hello, inc=1, device_id=(1, mine), device_id_type=MESH)

    @pl.when(me == 1)
    def _():
        pl.semaphore_wait(hello, 1)

    c_copy = pltpu.make_async_remote_copy(
        src_ref=c_hbm.at[:, :, other_bands], dst_ref=y0.at[my_rows],
        send_sem=c_send, recv_sem=c_recv, device_id=(other, mine), device_id_type=MESH)
    c_copy.start()

    @pl.when(me == 1)
    def _():
        for i in range(1, peers):
            pl.semaphore_signal(barrier, inc=1, device_id=(1, lax.rem(mine + i, peers)), device_id_type=MESH)

    groups = classes_of((True, True, True))
    n = len(groups)

    def place(g):
        total = 0
        for c in range(1, n):
            total = total + jnp.where(nb_ref[0, groups[c][0]] == g, c, 0)
        return lax.rem(total, n)

    nb_load.wait()
    spots = [place(g) for g in range(elems)]

    def collapse(i, e, at, rows):
        loads[i].wait()
        here = slice(at, at + rows)
        for c, group in enumerate(groups):
            total = hraw[e, group[0], here].astype(jnp.float32)
            for k in group[1:]:
                total = total + hraw[e, k, here].astype(jnp.float32)
            hsum[e, c, here] = (total + total).astype(jnp.bfloat16)
        mine_spot = place(me * local + e)
        for g in range(elems):
            hd[me * local + e, here, g * nb:(g + 1) * nb] = hsum[e, mine_spot ^ spots[g], here]

    h_copies = []
    for i, (e, at, rows) in enumerate(cuts):
        collapse(i, e, at, rows)
        copy = pltpu.make_async_remote_copy(
            src_ref=hd.at[me * local + e, pl.ds(at, rows)], dst_ref=hd.at[me * local + e, pl.ds(at, rows)],
            send_sem=h_send.at[i], recv_sem=h_recv.at[i], device_id=(other, mine), device_id_type=MESH)
        copy.start()
        h_copies.append(copy)
    for copy in b_loads:
        copy.start()
    t_copy = pltpu.make_async_remote_copy(
        src_ref=b_hbm.at[:, pl.ds(0, points)], dst_ref=near,
        send_sem=t_send, recv_sem=t_recv, device_id=(1, mine), device_id_type=MESH)
    n_load = pltpu.make_async_copy(b_hbm.at[:, pl.ds(0, points)], near, load_sem.at[2 * local + 1])

    @pl.when(me == 0)
    def _():
        t_copy.start()
        n_load.start()

    c_load.wait()
    c_copy.wait_recv()

    y, z = (y0, y1), (z0, z1)

    def product(source, at, count):
        left = hd[at].reshape(count * nb, elems * nb)
        right = y[source][...].reshape(elems * nb, half)
        out = jnp.dot(left, right, preferred_element_type=jnp.float32)
        return out.reshape(count, nb, half)

    def begin(at, count):
        rows = pl.ds(at, count)
        first = 0.5 * product(0, rows, count)
        z1[rows] = first
        y1[rows] = first.astype(jnp.bfloat16)

    begin(me * local, local)
    for e in range(0, local, STEP):
        for copy, cut in zip(h_copies, cuts):
            if e <= cut[0] < e + STEP:
                copy.wait_recv()
        begin(other * local + e, STEP)
    for step in range(1, CHEB - 1):
        now, later = step % 2, (step + 1) % 2
        for which in (slice(0, local), slice(local, elems)):
            before = y0[which].astype(jnp.float32) if step == 1 else z[later][which]
            following = product(now, which, local) - before
            if step < CHEB - 2:
                z[later][which] = following
            y[later][which] = following.astype(jnp.bfloat16)

    def early_terms():
        for e in range(local):
            orbital = jnp.dot(near[e], fall[e], preferred_element_type=jnp.float32)
            squares = sum(orbital[:, at:at + 128] * orbital[:, at:at + 128] for at in range(0, half, 128))
            sums = jnp.sum(squares.reshape(points // 128, 128, 128), axis=2)
            for r in range(points // 128):
                early[e:e + 1, r * 128:(r + 1) * 128] = sums[r:r + 1]

    e_slot = me * peers + mine
    e_copy = pltpu.make_async_remote_copy(
        src_ref=early, dst_ref=ebuf.at[e_slot], send_sem=e_send, recv_sem=e_recv,
        device_id=(0, 0), device_id_type=MESH)

    @pl.when(me == 0)
    def _():
        n_load.wait()

    @pl.when(me == 1)
    def _():
        t_copy.wait_recv()

    now, later = (CHEB - 1) % 2, CHEB % 2
    f_copy = pltpu.make_async_remote_copy(
        src_ref=fall.at[other_rows], dst_ref=frecv, send_sem=f_send, recv_sem=f_recv,
        device_id=(other, mine), device_id_type=MESH)
    def last_step(rows):
        fall[rows] = (product(now, rows, local) - z[later][rows]).astype(jnp.bfloat16)

    last_step(other_rows)
    f_copy.start()

    @pl.when(me == 1)
    def _():
        early_terms()
        pl.semaphore_wait(barrier, peers - 1)
        pl.semaphore_signal(ready, inc=1, device_id=(0, mine), device_id_type=MESH)
        e_copy.start()

    last_step(my_rows)

    @pl.when(me == 0)
    def _():
        early_terms()
        pl.semaphore_wait(ready, 1)

        @pl.when(mine != 0)
        def _():
            e_copy.start()

    f_ref[:, :, my_bands] = fall[my_rows]

    def gram(block):
        return lax.dot_general(block, block, (((1,), (1,)), ((), ())), preferred_element_type=jnp.float32)

    for copy in b_loads:
        copy.wait()
    grams = [gram(fall[me * local + e]) for e in range(local)]
    gblock[...] = jnp.zeros(gblock.shape, gblock.dtype)
    pick = (lax.broadcasted_iota(jnp.int32, (8, 2 * nb), 0)
            == lax.broadcasted_iota(jnp.int32, (8, 2 * nb), 1) // nb).astype(jnp.bfloat16)

    def terms(values, block, pair, store):
        size = values.shape[0]
        moved = jnp.dot(values, block, preferred_element_type=jnp.float32)
        products = moved * values.astype(jnp.float32)
        if pair % 2:
            sums = lax.dot_general(pick, products.astype(jnp.bfloat16), (((1,), (1,)), ((), ())),
                                   preferred_element_type=jnp.float32)
            for column in range(0, size, points):
                store(column, slice(2 * pair, 2 * pair + 2), slice(0, points), sums[:2, column:column + points])
            return
        for k in range(2):
            sums = jnp.sum(products[:, k * nb:(k + 1) * nb].reshape(size // 128, 128, nb), axis=2)
            for r in range(size // 128):
                column = r * 128 // points * points
                store(column, slice(2 * pair + k, 2 * pair + k + 1),
                      slice(r * 128 - column, r * 128 - column + 128), sums[r:r + 1])

    def first_terms():
        def store(column, rows, columns, value):
            ahead[rows, columns] = value
        for pair in range(local // 2):
            terms(basis[pair, pl.ds(0, points)], gblock[pair], pair, store)

    def group_terms(group):
        size = plane * points
        at = pl.ds(pl.multiple_of(group * size, size), size)

        def store(column, rows, columns, value):
            part[group * plane + column // points, rows, columns] = value
        for pair in range(local // 2):
            terms(basis[pair, at], gblock[pair], pair, store)

    def d_copy(i, source=None):
        target = lax.rem(mine + i, peers)
        return pltpu.make_async_remote_copy(
            src_ref=part.at[target] if source is None else source, dst_ref=rbuf.at[i], send_sem=d_send, recv_sem=d_recv,
            device_id=(me, target), device_id_type=MESH)

    f_copy.wait_recv()
    f_ref[:, :, other_bands] = frecv[...]
    for e in range(local):
        at = pl.ds(e % 2 * nb, nb)
        gblock[e // 2, at, at] = (grams[e] + gram(frecv[e])).astype(jnp.bfloat16)

    @pl.when(me == 1)
    def _():
        first_terms()

        @pl.when(mine != 0)
        def _():
            d_copy(peers - mine, ahead).start()

    planes = peers // plane
    own = mine // plane
    for turn in range(planes):
        up = jnp.where(turn < planes - 1 - own, planes - 1 - turn, turn - (planes - 1 - own))
        down = jnp.where(turn < own, turn, planes - 1 - (turn - own))
        group = own if turn == planes - 1 else jnp.where(2 * own < planes, up, down)
        group_terms(group)
        for d in range(1 if turn == planes - 1 else 0, plane):
            target = group * plane + lax.rem(mine + d, plane)

            @pl.when(target != 0)
            def _(target=target):
                d_copy(lax.rem(target - mine + peers, peers)).start()
    def wait_for(slots, sem):
        pltpu.make_async_copy(slots, slots, sem).wait()

    def added(terms):
        while len(terms) > 1:
            terms = [sum(terms[i:i + 2]) for i in range(0, len(terms), 2)]
        return terms[0]

    c_copy.wait_send()
    for copy in h_copies:
        copy.wait_send()
    f_copy.wait_send()

    @pl.when(me == 0)
    def _():
        t_copy.wait_send()

    wait_for(rbuf.at[pl.ds(1, peers - 2)], d_send)

    @pl.when((e_slot == 0) | (me == 1))
    def _():
        wait_for(rbuf.at[0], d_send)

    @pl.when(e_slot == 0)
    def _():
        wait_for(ebuf.at[pl.ds(1, 2 * peers - 1)], e_recv)
        d_ref[...] = added([early[...]] + [ebuf[i] for i in range(1, 2 * peers)]) / bands

    @pl.when(e_slot != 0)
    def _():
        e_copy.wait_send()
        wait_for(rbuf.at[pl.ds(1, peers - 1)], d_recv)
        d_ref[...] = added([part[mine]] + [rbuf[i] for i in range(1, peers)]) / bands


def deliver(f_in, d_in, f_hbm, d_hbm, sem):
    copies = [pltpu.make_async_copy(f_in, f_hbm, sem.at[0]), pltpu.make_async_copy(d_in, d_hbm, sem.at[1])]
    for copy in copies:
        copy.start()
    for copy in copies:
        copy.wait()


def quick(coefficients, hamiltonian, neighbours, basis_values, peers, bands):
    local, nb, width = coefficients.shape
    half = width // 2
    elems = 2 * local
    points = basis_values.shape[1]
    share = points // peers
    plane = 4 if peers % 4 == 0 else 1
    bf16, f32, dma = jnp.bfloat16, jnp.float32, pltpu.SemaphoreType.DMA
    grant = 67043328 - 2 * local * nb * width - 4 * local * share
    filtered, density = pl.pallas_call(
        functools.partial(fused, peers, bands, plane),
        out_shape=(pltpu.VMEM((local, nb, width), bf16), pltpu.VMEM((local, share), f32)),
        in_specs=[pl.BlockSpec(memory_space=pltpu.HBM)] * 4,
        out_specs=(pl.BlockSpec(memory_space=pltpu.VMEM), pl.BlockSpec(memory_space=pltpu.VMEM)),
        scratch_shapes=[
            pltpu.VMEM((local, OFFSETS, nb, nb), bf16),
            pltpu.VMEM((local, 8, nb, nb), bf16),
            pltpu.VMEM((elems, nb, elems * nb), bf16),
            pltpu.VMEM((elems, nb, half), bf16),
            pltpu.VMEM((elems, nb, half), bf16),
            pltpu.VMEM((elems, nb, half), f32),
            pltpu.VMEM((elems, nb, half), f32),
            pltpu.VMEM((elems, nb, half), bf16),
            pltpu.VMEM((local, nb, half), bf16),
            pltpu.VMEM((local // 2, points, 2 * nb), bf16),
            pltpu.VMEM((local, share, nb), bf16),
            pltpu.VMEM((local // 2, 2 * nb, 2 * nb), bf16),
            pltpu.VMEM((peers, local, share), f32),
            pltpu.VMEM((local, share), f32),
            pltpu.VMEM((local, share), f32),
            pltpu.VMEM((peers, local, share), f32),
            pltpu.VMEM((2 * peers, local, share), f32),
            pltpu.SMEM(neighbours.shape, jnp.int32),
            pltpu.SemaphoreType.REGULAR, pltpu.SemaphoreType.REGULAR,
            dma,
            dma((2 * local + 2,)),
            dma, dma,
            dma((len(chunks_of(local, nb)),)), dma((len(chunks_of(local, nb)),)), dma((len(chunks_of(local, nb)),)),
            dma, dma,
            dma, dma,
            dma, dma,
            dma, dma,
        ],
        compiler_params=pltpu.CompilerParams(
            collective_id=0, has_side_effects=True, vmem_limit_bytes=grant),
    )(neighbours, coefficients, hamiltonian, basis_values)
    return pl.pallas_call(
        deliver,
        out_shape=(jax.ShapeDtypeStruct((local, nb, width), bf16), jax.ShapeDtypeStruct((local, share), f32)),
        in_specs=[pl.BlockSpec(memory_space=pltpu.VMEM)] * 2,
        out_specs=(pl.BlockSpec(memory_space=pl.ANY), pl.BlockSpec(memory_space=pl.ANY)),
        scratch_shapes=[dma((2,))],
        compiler_params=pltpu.CompilerParams(vmem_limit_bytes=4 * 2**20),
    )(filtered, density)


def solution(mesh):
    split, peers = mesh.shape["elem"], mesh.shape["band"]

    def local(coefficients, hamiltonian, neighbours, basis_values):
        count, nb, width = coefficients.shape
        bands = width * peers
        fits = (split == 2 and peers > 2 and count * split == 8 and nb == 128 and width % 256 == 0
                and basis_values.shape[1] % (128 * peers) == 0)
        if fits:
            return quick(coefficients, hamiltonian, neighbours, basis_values, peers, bands)
        return plain(coefficients, hamiltonian, neighbours, basis_values, bands)

    return jax.shard_map(
        local,
        mesh=mesh,
        in_specs=(
            P("elem", None, "band"),
            P("elem", None, None, None),
            P("elem", None),
            P("elem", None, None),
        ),
        out_specs=(P("elem", None, "band"), P("elem", "band")),
        check_vma=False,
    )
```

```python
import functools

import jax
import jax.numpy as jnp
from jax import lax
from jax.experimental import pallas as pl
from jax.experimental.pallas import tpu as pltpu
from jax.sharding import PartitionSpec as P

CHEB = 6
OFFSETS = 27
STEP = 1
SPLIT = 2
MESH = pl.DeviceIdType.MESH


def classes_of(folded):
    groups = {}
    for k in range(OFFSETS):
        shift = (k // 9 - 1, k // 3 % 3 - 1, k % 3 - 1)
        key = tuple(s % 2 if f else s + 1 for s, f in zip(shift, folded))
        groups.setdefault(key, []).append(k)
    return [groups[key] for key in sorted(groups)]


def chunks_of(local, nb):
    return [(e, at, nb // n) for e in range(local) for n in [SPLIT if e == 0 else 1] for at in range(0, nb, nb // n)]


def plain(coefficients, hamiltonian, neighbours, basis_values, bands):
    groups = classes_of((False, True, True))
    wide = hamiltonian.astype(jnp.float32)
    blocks = jnp.stack([sum(wide[:, k] for k in g) for g in groups], axis=1).astype(jnp.bfloat16)
    index = jnp.stack([neighbours[:, g[0]] for g in groups], axis=1)

    def apply_operator(current):
        everyone = lax.all_gather(current, "elem", axis=0, tiled=True)
        return jnp.einsum("ekij,ekjb->eib", blocks, everyone[index], preferred_element_type=jnp.float32)

    previous = coefficients.astype(jnp.float32)
    current = apply_operator(coefficients)
    for _ in range(CHEB - 1):
        following = 2.0 * apply_operator(current.astype(jnp.bfloat16)) - previous
        previous, current = current, following
    filtered = current.astype(jnp.bfloat16)
    orbital = jnp.einsum("epj,ejb->epb", basis_values, filtered, preferred_element_type=jnp.float32)
    terms = jnp.sum(orbital * orbital, axis=2)
    summed = lax.psum_scatter(terms, "band", scatter_dimension=1, tiled=True)
    return filtered, summed / bands


def fused(peers, bands, plane, nb_hbm, c_hbm, h_hbm, b_hbm, f_ref, d_ref,
          hraw, hsum, hd, y0, y1, z0, z1, fall, frecv, basis, near, gblock, part, early, ahead, rbuf, ebuf, nb_ref,
          hello, ready, nb_sem, load_sem, c_send, c_recv, h_load, h_send, h_recv, f_send, f_recv, t_send, t_recv,
          d_send, d_recv, e_send, e_recv):
    me = lax.axis_index("elem")
    mine = lax.axis_index("band")
    other = 1 - me
    local, nb, width = c_hbm.shape
    half = width // 2
    elems = 2 * local
    points = b_hbm.shape[1] // peers

    my_rows = pl.ds(me * local, local)
    other_rows = pl.ds(other * local, local)
    my_bands = pl.ds(pl.multiple_of(me * half, half), half)
    other_bands = pl.ds(pl.multiple_of(other * half, half), half)

    cuts = chunks_of(local, nb)
    loads = [pltpu.make_async_copy(h_hbm.at[e, :, pl.ds(at, rows)], hraw.at[e, :, pl.ds(at, rows)], h_load.at[i])
             for i, (e, at, rows) in enumerate(cuts)]
    loads[0].start()
    nb_load = pltpu.make_async_copy(nb_hbm, nb_ref, nb_sem)
    nb_load.start()
    for copy in loads[1:]:
        copy.start()
    c_load = pltpu.make_async_copy(c_hbm.at[:, :, my_bands], y0.at[my_rows], load_sem.at[0])
    c_load.start()
    b_loads = [pltpu.make_async_copy(b_hbm.at[e], basis.at[e // 2, :, pl.ds(e % 2 * nb, nb)], load_sem.at[1]) for e in range(local)]

    def wait_for(slots, sem):
        pltpu.make_async_copy(slots, slots, sem).wait()

    barrier = pltpu.get_barrier_semaphore()

    @pl.when(me == 1)
    def _():
        pl.semaphore_signal(barrier, inc=1, device_id=(0, mine), device_id_type=MESH)

    @pl.when(me == 0)
    def _():
        pl.semaphore_wait(barrier, 1)
        pl.semaphore_signal(hello, inc=1, device_id=(1, mine), device_id_type=MESH)

    @pl.when(me == 1)
    def _():
        pl.semaphore_wait(hello, 1)

    c_copy = pltpu.make_async_remote_copy(
        src_ref=c_hbm.at[:, :, other_bands], dst_ref=y0.at[my_rows],
        send_sem=c_send, recv_sem=c_recv, device_id=(other, mine), device_id_type=MESH)
    c_copy.start()

    @pl.when(me == 1)
    def _():
        for i in range(1, peers):
            pl.semaphore_signal(barrier, inc=1, device_id=(1, lax.rem(mine + i, peers)), device_id_type=MESH)

    groups = classes_of((True, True, True))
    n = len(groups)

    def place(g):
        total = 0
        for c in range(1, n):
            total = total + jnp.where(nb_ref[0, groups[c][0]] == g, c, 0)
        return lax.rem(total, n)

    nb_load.wait()
    spots = [place(g) for g in range(elems)]

    def collapse(i, e, at, rows):
        loads[i].wait()
        here = slice(at, at + rows)
        for c, group in enumerate(groups):
            total = hraw[e, group[0], here].astype(jnp.float32)
            for k in group[1:]:
                total = total + hraw[e, k, here].astype(jnp.float32)
            hsum[e, c, here] = (total + total).astype(jnp.bfloat16)
        mine_spot = place(me * local + e)
        for g in range(elems):
            hd[me * local + e, here, g * nb:(g + 1) * nb] = hsum[e, mine_spot ^ spots[g], here]

    h_copies = []
    for i, (e, at, rows) in enumerate(cuts):
        collapse(i, e, at, rows)
        copy = pltpu.make_async_remote_copy(
            src_ref=hd.at[me * local + e, pl.ds(at, rows)], dst_ref=hd.at[me * local + e, pl.ds(at, rows)],
            send_sem=h_send, recv_sem=h_recv.at[i], device_id=(other, mine), device_id_type=MESH)
        copy.start()
        h_copies.append(copy)
    for copy in b_loads:
        copy.start()
    t_copy = pltpu.make_async_remote_copy(
        src_ref=b_hbm.at[:, pl.ds(0, points)], dst_ref=near,
        send_sem=t_send, recv_sem=t_recv, device_id=(1, mine), device_id_type=MESH)
    n_load = pltpu.make_async_copy(b_hbm.at[:, pl.ds(0, points)], near, load_sem.at[2])

    @pl.when(me == 0)
    def _():
        t_copy.start()
        n_load.start()

    c_load.wait()
    c_copy.wait_recv()

    y, z = (y0, y1), (z0, z1)

    def product(source, at, count):
        left = hd[at].reshape(count * nb, elems * nb)
        right = y[source][...].reshape(elems * nb, half)
        out = jnp.dot(left, right, preferred_element_type=jnp.float32)
        return out.reshape(count, nb, half)

    def begin(at, count):
        rows = pl.ds(at, count)
        first = 0.5 * product(0, rows, count)
        z1[rows] = first
        y1[rows] = first.astype(jnp.bfloat16)

    begin(me * local, local)
    for e in range(0, local, STEP):
        for copy, cut in zip(h_copies, cuts):
            if e <= cut[0] < e + STEP:
                copy.wait_recv()
        begin(other * local + e, STEP)
    for step in range(1, CHEB - 1):
        now, later = step % 2, (step + 1) % 2
        for which in (slice(0, local), slice(local, elems)):
            before = y0[which].astype(jnp.float32) if step == 1 else z[later][which]
            following = product(now, which, local) - before
            if step < CHEB - 2:
                z[later][which] = following
            y[later][which] = following.astype(jnp.bfloat16)

    def early_terms():
        for e in range(local):
            orbital = jnp.dot(near[e], fall[e], preferred_element_type=jnp.float32)
            squares = sum(orbital[:, at:at + 128] * orbital[:, at:at + 128] for at in range(0, half, 128))
            sums = jnp.sum(squares.reshape(points // 128, 128, 128), axis=2)
            for r in range(points // 128):
                early[e:e + 1, r * 128:(r + 1) * 128] = sums[r:r + 1]

    e_slot = me * peers + mine
    e_copy = pltpu.make_async_remote_copy(
        src_ref=early, dst_ref=ebuf.at[e_slot], send_sem=e_send, recv_sem=e_recv,
        device_id=(0, 0), device_id_type=MESH)

    @pl.when(me == 0)
    def _():
        n_load.wait()

    @pl.when(me == 1)
    def _():
        t_copy.wait_recv()

    now, later = (CHEB - 1) % 2, CHEB % 2
    f_copy = pltpu.make_async_remote_copy(
        src_ref=fall.at[other_rows], dst_ref=frecv, send_sem=f_send, recv_sem=f_recv,
        device_id=(other, mine), device_id_type=MESH)
    def last_step(rows):
        fall[rows] = (product(now, rows, local) - z[later][rows]).astype(jnp.bfloat16)

    last_step(other_rows)
    f_copy.start()

    @pl.when(me == 1)
    def _():
        early_terms()
        pl.semaphore_wait(barrier, peers - 1)
        pl.semaphore_signal(ready, inc=1, device_id=(0, mine), device_id_type=MESH)
        e_copy.start()

    last_step(my_rows)

    @pl.when(me == 0)
    def _():
        early_terms()
        pl.semaphore_wait(ready, 1)

        @pl.when(mine != 0)
        def _():
            e_copy.start()

    f_ref[:, :, my_bands] = fall[my_rows]

    def gram(block):
        return lax.dot_general(block, block, (((1,), (1,)), ((), ())), preferred_element_type=jnp.float32)

    wait_for(basis, load_sem.at[1])
    grams = [gram(fall[me * local + e]) for e in range(local)]
    gblock[...] = jnp.zeros(gblock.shape, gblock.dtype)
    pick = (lax.broadcasted_iota(jnp.int32, (8, 2 * nb), 0)
            == lax.broadcasted_iota(jnp.int32, (8, 2 * nb), 1) // nb).astype(jnp.bfloat16)

    def terms(values, block, pair, store):
        size = values.shape[0]
        moved = jnp.dot(values, block, preferred_element_type=jnp.float32)
        products = moved * values.astype(jnp.float32)
        if pair % 2:
            sums = lax.dot_general(pick, products.astype(jnp.bfloat16), (((1,), (1,)), ((), ())),
                                   preferred_element_type=jnp.float32)
            for column in range(0, size, points):
                store(column, slice(2 * pair, 2 * pair + 2), slice(0, points), sums[:2, column:column + points])
            return
        for k in range(2):
            sums = jnp.sum(products[:, k * nb:(k + 1) * nb].reshape(size // 128, 128, nb), axis=2)
            for r in range(size // 128):
                column = r * 128 // points * points
                store(column, slice(2 * pair + k, 2 * pair + k + 1),
                      slice(r * 128 - column, r * 128 - column + 128), sums[r:r + 1])

    def first_terms():
        def store(column, rows, columns, value):
            ahead[rows, columns] = value
        for pair in range(local // 2):
            terms(basis[pair, pl.ds(0, points)], gblock[pair], pair, store)

    def group_terms(group):
        size = plane * points
        at = pl.ds(pl.multiple_of(group * size, size), size)

        def store(column, rows, columns, value):
            part[group * plane + column // points, rows, columns] = value
        for pair in range(local // 2):
            terms(basis[pair, at], gblock[pair], pair, store)

    def d_copy(i, source=None):
        target = lax.rem(mine + i, peers)
        return pltpu.make_async_remote_copy(
            src_ref=part.at[target] if source is None else source, dst_ref=rbuf.at[i], send_sem=d_send, recv_sem=d_recv,
            device_id=(me, target), device_id_type=MESH)

    f_copy.wait_recv()
    f_ref[:, :, other_bands] = frecv[...]
    for e in range(local):
        at = pl.ds(e % 2 * nb, nb)
        gblock[e // 2, at, at] = (grams[e] + gram(frecv[e])).astype(jnp.bfloat16)

    @pl.when(me == 1)
    def _():
        first_terms()

        @pl.when(mine != 0)
        def _():
            d_copy(peers - mine, ahead).start()

    planes = peers // plane
    own = mine // plane
    for turn in range(planes):
        up = jnp.where(turn < planes - 1 - own, planes - 1 - turn, turn - (planes - 1 - own))
        down = jnp.where(turn < own, turn, planes - 1 - (turn - own))
        group = own if turn == planes - 1 else jnp.where(2 * own < planes, up, down)
        group_terms(group)
        for d in range(1 if turn == planes - 1 else 0, plane):
            target = group * plane + lax.rem(mine + d, plane)

            @pl.when(target != 0)
            def _(target=target):
                d_copy(lax.rem(target - mine + peers, peers)).start()
    def added(terms):
        while len(terms) > 1:
            terms = [sum(terms[i:i + 2]) for i in range(0, len(terms), 2)]
        return terms[0]

    c_copy.wait_send()
    wait_for(hd.at[my_rows], h_send)
    f_copy.wait_send()

    @pl.when(me == 0)
    def _():
        t_copy.wait_send()

    wait_for(rbuf.at[pl.ds(1, peers - 2)], d_send)

    @pl.when((e_slot == 0) | (me == 1))
    def _():
        wait_for(rbuf.at[0], d_send)

    @pl.when(e_slot == 0)
    def _():
        wait_for(ebuf.at[pl.ds(1, 2 * peers - 1)], e_recv)
        d_ref[...] = added([early[...]] + [ebuf[i] for i in range(1, 2 * peers)]) / bands

    @pl.when(e_slot != 0)
    def _():
        e_copy.wait_send()
        wait_for(rbuf.at[pl.ds(1, peers - 1)], d_recv)
        d_ref[...] = added([part[mine]] + [rbuf[i] for i in range(1, peers)]) / bands


def deliver(f_in, d_in, f_hbm, d_hbm, sem):
    copies = [pltpu.make_async_copy(f_in, f_hbm, sem.at[0]), pltpu.make_async_copy(d_in, d_hbm, sem.at[1])]
    for copy in copies:
        copy.start()
    for copy in copies:
        copy.wait()


def quick(coefficients, hamiltonian, neighbours, basis_values, peers, bands):
    local, nb, width = coefficients.shape
    half = width // 2
    elems = 2 * local
    points = basis_values.shape[1]
    share = points // peers
    plane = 4 if peers % 4 == 0 else 1
    bf16, f32, dma = jnp.bfloat16, jnp.float32, pltpu.SemaphoreType.DMA
    grant = 67043328 - 2 * local * nb * width - 4 * local * share
    filtered, density = pl.pallas_call(
        functools.partial(fused, peers, bands, plane),
        out_shape=(pltpu.VMEM((local, nb, width), bf16), pltpu.VMEM((local, share), f32)),
        in_specs=[pl.BlockSpec(memory_space=pltpu.HBM)] * 4,
        out_specs=(pl.BlockSpec(memory_space=pltpu.VMEM), pl.BlockSpec(memory_space=pltpu.VMEM)),
        scratch_shapes=[
            pltpu.VMEM((local, OFFSETS, nb, nb), bf16),
            pltpu.VMEM((local, 8, nb, nb), bf16),
            pltpu.VMEM((elems, nb, elems * nb), bf16),
            pltpu.VMEM((elems, nb, half), bf16),
            pltpu.VMEM((elems, nb, half), bf16),
            pltpu.VMEM((elems, nb, half), f32),
            pltpu.VMEM((elems, nb, half), f32),
            pltpu.VMEM((elems, nb, half), bf16),
            pltpu.VMEM((local, nb, half), bf16),
            pltpu.VMEM((local // 2, points, 2 * nb), bf16),
            pltpu.VMEM((local, share, nb), bf16),
            pltpu.VMEM((local // 2, 2 * nb, 2 * nb), bf16),
            pltpu.VMEM((peers, local, share), f32),
            pltpu.VMEM((local, share), f32),
            pltpu.VMEM((local, share), f32),
            pltpu.VMEM((peers, local, share), f32),
            pltpu.VMEM((2 * peers, local, share), f32),
            pltpu.SMEM(neighbours.shape, jnp.int32),
            pltpu.SemaphoreType.REGULAR, pltpu.SemaphoreType.REGULAR,
            dma,
            dma((3,)),
            dma, dma,
            dma((len(chunks_of(local, nb)),)), dma, dma((len(chunks_of(local, nb)),)),
            dma, dma,
            dma, dma,
            dma, dma,
            dma, dma,
        ],
        compiler_params=pltpu.CompilerParams(
            collective_id=0, has_side_effects=True, vmem_limit_bytes=grant),
    )(neighbours, coefficients, hamiltonian, basis_values)
    return pl.pallas_call(
        deliver,
        out_shape=(jax.ShapeDtypeStruct((local, nb, width), bf16), jax.ShapeDtypeStruct((local, share), f32)),
        in_specs=[pl.BlockSpec(memory_space=pltpu.VMEM)] * 2,
        out_specs=(pl.BlockSpec(memory_space=pl.ANY), pl.BlockSpec(memory_space=pl.ANY)),
        scratch_shapes=[dma((2,))],
        compiler_params=pltpu.CompilerParams(vmem_limit_bytes=4 * 2**20),
    )(filtered, density)


def solution(mesh):
    split, peers = mesh.shape["elem"], mesh.shape["band"]

    def local(coefficients, hamiltonian, neighbours, basis_values):
        count, nb, width = coefficients.shape
        bands = width * peers
        fits = (split == 2 and peers > 2 and count * split == 8 and nb == 128 and width % 256 == 0
                and basis_values.shape[1] % (128 * peers) == 0)
        if fits:
            return quick(coefficients, hamiltonian, neighbours, basis_values, peers, bands)
        return plain(coefficients, hamiltonian, neighbours, basis_values, bands)

    return jax.shard_map(
        local,
        mesh=mesh,
        in_specs=(
            P("elem", None, "band"),
            P("elem", None, None, None),
            P("elem", None),
            P("elem", None, None),
        ),
        out_specs=(P("elem", None, "band"), P("elem", "band")),
        check_vma=False,
    )
```

```python
import functools

import jax
import jax.numpy as jnp
from jax import lax
from jax.experimental import pallas as pl
from jax.experimental.pallas import tpu as pltpu
from jax.sharding import PartitionSpec as P

CHEB = 6
OFFSETS = 27
STEP = 1
SPLIT = 2
MESH = pl.DeviceIdType.MESH


def classes_of(folded):
    groups = {}
    for k in range(OFFSETS):
        shift = (k // 9 - 1, k // 3 % 3 - 1, k % 3 - 1)
        key = tuple(s % 2 if f else s + 1 for s, f in zip(shift, folded))
        groups.setdefault(key, []).append(k)
    return [groups[key] for key in sorted(groups)]


def chunks_of(local, nb):
    return [(e, at, nb // n) for e in range(local) for n in [SPLIT if e == 0 else 1] for at in range(0, nb, nb // n)]


def plain(coefficients, hamiltonian, neighbours, basis_values, bands):
    groups = classes_of((False, True, True))
    wide = hamiltonian.astype(jnp.float32)
    blocks = jnp.stack([sum(wide[:, k] for k in g) for g in groups], axis=1).astype(jnp.bfloat16)
    index = jnp.stack([neighbours[:, g[0]] for g in groups], axis=1)

    def apply_operator(current):
        everyone = lax.all_gather(current, "elem", axis=0, tiled=True)
        return jnp.einsum("ekij,ekjb->eib", blocks, everyone[index], preferred_element_type=jnp.float32)

    previous = coefficients.astype(jnp.float32)
    current = apply_operator(coefficients)
    for _ in range(CHEB - 1):
        following = 2.0 * apply_operator(current.astype(jnp.bfloat16)) - previous
        previous, current = current, following
    filtered = current.astype(jnp.bfloat16)
    orbital = jnp.einsum("epj,ejb->epb", basis_values, filtered, preferred_element_type=jnp.float32)
    terms = jnp.sum(orbital * orbital, axis=2)
    summed = lax.psum_scatter(terms, "band", scatter_dimension=1, tiled=True)
    return filtered, summed / bands


def fused(peers, bands, plane, nb_hbm, c_hbm, h_hbm, b_hbm, f_ref, d_ref,
          hraw, hsum, hd, y0, y1, z0, z1, fall, frecv, basis, near, gblock, part, early, ahead, rbuf, ebuf, nb_ref,
          hello, ready, nb_sem, load_sem, c_send, c_recv, h_load, h_send, h_recv, f_send, f_recv, t_send, t_recv,
          d_send, d_recv, e_send, e_recv):
    me = lax.axis_index("elem")
    mine = lax.axis_index("band")
    other = 1 - me
    local, nb, width = c_hbm.shape
    half = width // 2
    elems = 2 * local
    points = b_hbm.shape[1] // peers

    my_rows = pl.ds(me * local, local)
    other_rows = pl.ds(other * local, local)
    my_bands = pl.ds(pl.multiple_of(me * half, half), half)
    other_bands = pl.ds(pl.multiple_of(other * half, half), half)

    cuts = chunks_of(local, nb)
    loads = [pltpu.make_async_copy(h_hbm.at[e, :, pl.ds(at, rows)], hraw.at[e, :, pl.ds(at, rows)], h_load.at[i])
             for i, (e, at, rows) in enumerate(cuts)]
    loads[0].start()
    nb_load = pltpu.make_async_copy(nb_hbm, nb_ref, nb_sem)
    nb_load.start()
    c_load = pltpu.make_async_copy(c_hbm.at[:, :, my_bands], y0.at[my_rows], load_sem.at[0])
    c_load.start()
    for copy in loads[1:]:
        copy.start()
    b_loads = [pltpu.make_async_copy(b_hbm.at[e], basis.at[e // 2, :, pl.ds(e % 2 * nb, nb)], load_sem.at[1]) for e in range(local)]

    def wait_for(slots, sem):
        pltpu.make_async_copy(slots, slots, sem).wait()

    barrier = pltpu.get_barrier_semaphore()

    @pl.when(me == 1)
    def _():
        pl.semaphore_signal(barrier, inc=1, device_id=(0, mine), device_id_type=MESH)

    @pl.when(me == 0)
    def _():
        pl.semaphore_wait(barrier, 1)
        pl.semaphore_signal(hello, inc=1, device_id=(1, mine), device_id_type=MESH)

    @pl.when(me == 1)
    def _():
        pl.semaphore_wait(hello, 1)

    c_copy = pltpu.make_async_remote_copy(
        src_ref=c_hbm.at[:, :, other_bands], dst_ref=y0.at[my_rows],
        send_sem=c_send, recv_sem=c_recv, device_id=(other, mine), device_id_type=MESH)
    c_copy.start()

    @pl.when(me == 1)
    def _():
        for i in range(1, peers):
            pl.semaphore_signal(barrier, inc=1, device_id=(1, lax.rem(mine + i, peers)), device_id_type=MESH)

    groups = classes_of((True, True, True))
    n = len(groups)

    def place(g):
        total = 0
        for c in range(1, n):
            total = total + jnp.where(nb_ref[0, groups[c][0]] == g, c, 0)
        return lax.rem(total, n)

    nb_load.wait()
    spots = [place(g) for g in range(elems)]

    def collapse(i, e, at, rows):
        loads[i].wait()
        here = slice(at, at + rows)
        for c, group in enumerate(groups):
            total = hraw[e, group[0], here].astype(jnp.float32)
            for k in group[1:]:
                total = total + hraw[e, k, here].astype(jnp.float32)
            hsum[e, c, here] = (total + total).astype(jnp.bfloat16)
        mine_spot = place(me * local + e)
        for g in range(elems):
            hd[me * local + e, here, g * nb:(g + 1) * nb] = hsum[e, mine_spot ^ spots[g], here]

    h_copies = []
    for i, (e, at, rows) in enumerate(cuts):
        collapse(i, e, at, rows)
        copy = pltpu.make_async_remote_copy(
            src_ref=hd.at[me * local + e, pl.ds(at, rows)], dst_ref=hd.at[me * local + e, pl.ds(at, rows)],
            send_sem=h_send, recv_sem=h_recv.at[i], device_id=(other, mine), device_id_type=MESH)
        copy.start()
        h_copies.append(copy)
    for copy in b_loads:
        copy.start()
    t_copy = pltpu.make_async_remote_copy(
        src_ref=b_hbm.at[:, pl.ds(0, points)], dst_ref=near,
        send_sem=t_send, recv_sem=t_recv, device_id=(1, mine), device_id_type=MESH)
    n_load = pltpu.make_async_copy(b_hbm.at[:, pl.ds(0, points)], near, load_sem.at[2])

    @pl.when(me == 0)
    def _():
        t_copy.start()
        n_load.start()

    c_load.wait()
    c_copy.wait_recv()

    y, z = (y0, y1), (z0, z1)

    def product(source, at, count):
        left = hd[at].reshape(count * nb, elems * nb)
        right = y[source][...].reshape(elems * nb, half)
        out = jnp.dot(left, right, preferred_element_type=jnp.float32)
        return out.reshape(count, nb, half)

    def begin(at, count):
        rows = pl.ds(at, count)
        first = 0.5 * product(0, rows, count)
        z1[rows] = first
        y1[rows] = first.astype(jnp.bfloat16)

    begin(me * local, local)
    for e in range(0, local, STEP):
        for copy, cut in zip(h_copies, cuts):
            if e <= cut[0] < e + STEP:
                copy.wait_recv()
        begin(other * local + e, STEP)
    for step in range(1, CHEB - 1):
        now, later = step % 2, (step + 1) % 2
        for which in (slice(0, local), slice(local, elems)):
            before = y0[which].astype(jnp.float32) if step == 1 else z[later][which]
            following = product(now, which, local) - before
            if step < CHEB - 2:
                z[later][which] = following
            y[later][which] = following.astype(jnp.bfloat16)

    def early_terms():
        for e in range(local):
            orbital = jnp.dot(near[e], fall[e], preferred_element_type=jnp.float32)
            squares = sum(orbital[:, at:at + 128] * orbital[:, at:at + 128] for at in range(0, half, 128))
            sums = jnp.sum(squares.reshape(points // 128, 128, 128), axis=2)
            for r in range(points // 128):
                early[e:e + 1, r * 128:(r + 1) * 128] = sums[r:r + 1]

    e_slot = me * peers + mine
    e_copy = pltpu.make_async_remote_copy(
        src_ref=early, dst_ref=ebuf.at[e_slot], send_sem=e_send, recv_sem=e_recv,
        device_id=(0, 0), device_id_type=MESH)

    @pl.when(me == 0)
    def _():
        n_load.wait()

    @pl.when(me == 1)
    def _():
        t_copy.wait_recv()

    now, later = (CHEB - 1) % 2, CHEB % 2
    f_copy = pltpu.make_async_remote_copy(
        src_ref=fall.at[other_rows], dst_ref=frecv, send_sem=f_send, recv_sem=f_recv,
        device_id=(other, mine), device_id_type=MESH)
    def last_step(rows):
        fall[rows] = (product(now, rows, local) - z[later][rows]).astype(jnp.bfloat16)

    last_step(other_rows)
    f_copy.start()

    @pl.when(me == 1)
    def _():
        early_terms()
        pl.semaphore_wait(barrier, peers - 1)
        pl.semaphore_signal(ready, inc=1, device_id=(0, mine), device_id_type=MESH)
        e_copy.start()

    last_step(my_rows)

    @pl.when(me == 0)
    def _():
        early_terms()
        pl.semaphore_wait(ready, 1)

        @pl.when(mine != 0)
        def _():
            e_copy.start()

    f_ref[:, :, my_bands] = fall[my_rows]

    def gram(block):
        return lax.dot_general(block, block, (((1,), (1,)), ((), ())), preferred_element_type=jnp.float32)

    wait_for(basis, load_sem.at[1])
    grams = [gram(fall[me * local + e]) for e in range(local)]
    gblock[...] = jnp.zeros(gblock.shape, gblock.dtype)
    pick = (lax.broadcasted_iota(jnp.int32, (8, 2 * nb), 0)
            == lax.broadcasted_iota(jnp.int32, (8, 2 * nb), 1) // nb).astype(jnp.bfloat16)

    def terms(values, block, pair, store):
        size = values.shape[0]
        moved = jnp.dot(values, block, preferred_element_type=jnp.float32)
        products = moved * values.astype(jnp.float32)
        if pair % 2:
            sums = lax.dot_general(pick, products.astype(jnp.bfloat16), (((1,), (1,)), ((), ())),
                                   preferred_element_type=jnp.float32)
            for column in range(0, size, points):
                store(column, slice(2 * pair, 2 * pair + 2), slice(0, points), sums[:2, column:column + points])
            return
        for k in range(2):
            sums = jnp.sum(products[:, k * nb:(k + 1) * nb].reshape(size // 128, 128, nb), axis=2)
            for r in range(size // 128):
                column = r * 128 // points * points
                store(column, slice(2 * pair + k, 2 * pair + k + 1),
                      slice(r * 128 - column, r * 128 - column + 128), sums[r:r + 1])

    def first_terms():
        def store(column, rows, columns, value):
            ahead[rows, columns] = value
        for pair in range(local // 2):
            terms(basis[pair, pl.ds(0, points)], gblock[pair], pair, store)

    def group_terms(group):
        size = plane * points
        at = pl.ds(pl.multiple_of(group * size, size), size)

        def store(column, rows, columns, value):
            part[group * plane + column // points, rows, columns] = value
        for pair in range(local // 2):
            terms(basis[pair, at], gblock[pair], pair, store)

    def d_copy(i, source=None):
        target = lax.rem(mine + i, peers)
        return pltpu.make_async_remote_copy(
            src_ref=part.at[target] if source is None else source, dst_ref=rbuf.at[i], send_sem=d_send, recv_sem=d_recv,
            device_id=(me, target), device_id_type=MESH)

    f_copy.wait_recv()
    f_ref[:, :, other_bands] = frecv[...]
    for e in range(local):
        at = pl.ds(e % 2 * nb, nb)
        gblock[e // 2, at, at] = (grams[e] + gram(frecv[e])).astype(jnp.bfloat16)

    @pl.when(me == 1)
    def _():
        first_terms()

        @pl.when(mine != 0)
        def _():
            d_copy(peers - mine, ahead).start()

    planes = peers // plane
    own = mine // plane
    for turn in range(planes):
        up = jnp.where(turn < planes - 1 - own, planes - 1 - turn, turn - (planes - 1 - own))
        down = jnp.where(turn < own, turn, planes - 1 - (turn - own))
        group = own if turn == planes - 1 else jnp.where(2 * own < planes, up, down)
        group_terms(group)
        for d in range(1 if turn == planes - 1 else 0, plane):
            target = group * plane + lax.rem(mine + d, plane)

            @pl.when(target != 0)
            def _(target=target):
                d_copy(lax.rem(target - mine + peers, peers)).start()
    def added(terms):
        while len(terms) > 1:
            terms = [sum(terms[i:i + 2]) for i in range(0, len(terms), 2)]
        return terms[0]

    c_copy.wait_send()
    wait_for(hd.at[my_rows], h_send)
    f_copy.wait_send()

    @pl.when(me == 0)
    def _():
        t_copy.wait_send()

    wait_for(rbuf.at[pl.ds(1, peers - 2)], d_send)

    @pl.when((e_slot == 0) | (me == 1))
    def _():
        wait_for(rbuf.at[0], d_send)

    @pl.when(e_slot == 0)
    def _():
        wait_for(ebuf.at[pl.ds(1, 2 * peers - 1)], e_recv)
        d_ref[...] = added([early[...]] + [ebuf[i] for i in range(1, 2 * peers)]) / bands

    @pl.when(e_slot != 0)
    def _():
        e_copy.wait_send()
        wait_for(rbuf.at[pl.ds(1, peers - 1)], d_recv)
        d_ref[...] = added([part[mine]] + [rbuf[i] for i in range(1, peers)]) / bands


def deliver(f_in, d_in, f_hbm, d_hbm, sem):
    copies = [pltpu.make_async_copy(f_in, f_hbm, sem.at[0]), pltpu.make_async_copy(d_in, d_hbm, sem.at[1])]
    for copy in copies:
        copy.start()
    for copy in copies:
        copy.wait()


def quick(coefficients, hamiltonian, neighbours, basis_values, peers, bands):
    local, nb, width = coefficients.shape
    half = width // 2
    elems = 2 * local
    points = basis_values.shape[1]
    share = points // peers
    plane = 4 if peers % 4 == 0 else 1
    bf16, f32, dma = jnp.bfloat16, jnp.float32, pltpu.SemaphoreType.DMA
    grant = 67043328 - 2 * local * nb * width - 4 * local * share
    filtered, density = pl.pallas_call(
        functools.partial(fused, peers, bands, plane),
        out_shape=(pltpu.VMEM((local, nb, width), bf16), pltpu.VMEM((local, share), f32)),
        in_specs=[pl.BlockSpec(memory_space=pltpu.HBM)] * 4,
        out_specs=(pl.BlockSpec(memory_space=pltpu.VMEM), pl.BlockSpec(memory_space=pltpu.VMEM)),
        scratch_shapes=[
            pltpu.VMEM((local, OFFSETS, nb, nb), bf16),
            pltpu.VMEM((local, 8, nb, nb), bf16),
            pltpu.VMEM((elems, nb, elems * nb), bf16),
            pltpu.VMEM((elems, nb, half), bf16),
            pltpu.VMEM((elems, nb, half), bf16),
            pltpu.VMEM((elems, nb, half), f32),
            pltpu.VMEM((elems, nb, half), f32),
            pltpu.VMEM((elems, nb, half), bf16),
            pltpu.VMEM((local, nb, half), bf16),
            pltpu.VMEM((local // 2, points, 2 * nb), bf16),
            pltpu.VMEM((local, share, nb), bf16),
            pltpu.VMEM((local // 2, 2 * nb, 2 * nb), bf16),
            pltpu.VMEM((peers, local, share), f32),
            pltpu.VMEM((local, share), f32),
            pltpu.VMEM((local, share), f32),
            pltpu.VMEM((peers, local, share), f32),
            pltpu.VMEM((2 * peers, local, share), f32),
            pltpu.SMEM(neighbours.shape, jnp.int32),
            pltpu.SemaphoreType.REGULAR, pltpu.SemaphoreType.REGULAR,
            dma,
            dma((3,)),
            dma, dma,
            dma((len(chunks_of(local, nb)),)), dma, dma((len(chunks_of(local, nb)),)),
            dma, dma,
            dma, dma,
            dma, dma,
            dma, dma,
        ],
        compiler_params=pltpu.CompilerParams(
            collective_id=0, has_side_effects=True, vmem_limit_bytes=grant),
    )(neighbours, coefficients, hamiltonian, basis_values)
    return pl.pallas_call(
        deliver,
        out_shape=(jax.ShapeDtypeStruct((local, nb, width), bf16), jax.ShapeDtypeStruct((local, share), f32)),
        in_specs=[pl.BlockSpec(memory_space=pltpu.VMEM)] * 2,
        out_specs=(pl.BlockSpec(memory_space=pl.ANY), pl.BlockSpec(memory_space=pl.ANY)),
        scratch_shapes=[dma((2,))],
        compiler_params=pltpu.CompilerParams(vmem_limit_bytes=4 * 2**20),
    )(filtered, density)


def solution(mesh):
    split, peers = mesh.shape["elem"], mesh.shape["band"]

    def local(coefficients, hamiltonian, neighbours, basis_values):
        count, nb, width = coefficients.shape
        bands = width * peers
        fits = (split == 2 and peers > 2 and count * split == 8 and nb == 128 and width % 256 == 0
                and basis_values.shape[1] % (128 * peers) == 0)
        if fits:
            return quick(coefficients, hamiltonian, neighbours, basis_values, peers, bands)
        return plain(coefficients, hamiltonian, neighbours, basis_values, bands)

    return jax.shard_map(
        local,
        mesh=mesh,
        in_specs=(
            P("elem", None, "band"),
            P("elem", None, None, None),
            P("elem", None),
            P("elem", None, None),
        ),
        out_specs=(P("elem", None, "band"), P("elem", "band")),
        check_vma=False,
    )
```
